256 devices in a mesh: grid: 64 (over z_hi, y, x, core), orb: 4 (over z_lo).
Axes of the slice: x: 4, y: 4, z: 8 (z_hi: 2, z_lo: 4; z = z_hi * 4 + z_lo), core: 2. Of those that a mesh axis runs over, the one named last changes fastest.
Arguments:
- psi_in: float32 [128, 384, 8, 128], P('orb', 'grid')
- v_local: float32 [384, 8, 128], P('grid'), may hold values from -3 to 0.5
- proj_index: int32 [192, 4, 128], P('grid'), may hold values from 0 to 6143
- proj_value: float32 [192, 4, 4, 128], P('grid'), may hold values from -1.2 to 1.2
- kb_energy: float32 [256, 4], P('grid'), may hold values from 0.5 to 3
Outputs:
- filtered: float32 [128, 384, 8, 128], P('orb', 'grid')
- gram: float32 [128, 128], P('orb', 'grid')
The draws below stay inside these ranges and needn't reach their ends.
All inputs are finite; a program needn't handle non-finite values.
Results may differ from the reference program's by a relative error of at most 0.00005.
Values sent between devices are 32-bit elements; how exact they have to be, the bound alone decides.
No kernel may reach another device: no remote copies, remote signals or barrier semaphores. Data moves between devices by JAX's collectives and lax.ppermute only.
A program may use at most 128 MiB of HBM per device.

```python
import jax
import jax.numpy as jnp
from jax import lax

NX = 128
NY = 8
NORB = 128
PROJ = 4
ATOM_SLOTS = 4
PTS = 128
NZ = 384
CELLS = 6144
PIECES = 192
ATOMS = 256
N_GRID = 64


def draw_psi_in(key, part):
    key_own = jax.random.fold_in(key, 11)
    key_shared = jax.random.fold_in(key, 12)
    key_weight = jax.random.fold_in(key, 13)
    own = jnp.clip(jax.random.normal(key_own, (NORB, NZ, NY, NX), jnp.float32), -5.0, 5.0)
    weight = jax.random.uniform(key_weight, (NORB, 1, 1, 1), jnp.float32, -1.0, 1.0)
    shared = jnp.clip(jax.random.normal(key_shared, (1, NZ, NY, NX), jnp.float32), -5.0, 5.0)
    return own + 0.8 * weight * shared


def with_ends(entries, own_key, low, top_value):
    extent = entries.shape
    place = [jax.random.randint(jax.random.fold_in(own_key, axis), (), 0, extent[axis]) for axis in range(len(extent))]
    entries = entries.at[tuple(place)].set(low)
    longest = extent.index(max(extent))
    place[longest] = (place[longest] + 1) % extent[longest]
    return entries.at[tuple(place)].set(top_value)


def block_levels(stream_key, dims, shards, least, largest):
    def one(dim, blocks):
        heights = jax.random.uniform(jax.random.fold_in(jax.random.fold_in(stream_key, 6), dim), (blocks,), jnp.float32, least / len(shards), largest / len(shards))
        return jnp.repeat(jnp.exp(heights), dims[dim] // blocks).reshape((-1,) + (1,) * (len(dims) - dim - 1))

    gain = one(*shards[0])
    for cut in shards[1:]:
        gain = gain * one(*cut)
    return gain


def centred(rng, extent, width, most, pieces=(), kind=jnp.bfloat16):
    drawn = width * jax.random.normal(rng, extent, jnp.float32)
    if pieces:
        drawn = drawn * block_levels(rng, extent, pieces, -0.22, 0.18)
    return jnp.clip(drawn, -most, most).astype(kind)


def setup_inputs(seed: int = 0) -> dict:
    seeds = jax.random.split(jax.random.key(seed), 6)
    psi_in = draw_psi_in(jax.random.fold_in(seeds[5], 71), 0)
    v_local = jnp.clip(-3.0 + 3.5 * jax.random.uniform(seeds[1], (NZ, NY, NX), jnp.float32) ** block_levels(seeds[1], (NZ, NY, NX), ((0, 64),), -0.2, 0.2), -3.0, 0.5)
    proj_index = with_ends(jax.random.randint(seeds[2], (PIECES, ATOM_SLOTS, PTS), 0, CELLS), jax.random.fold_in(seeds[2], 1), 0, CELLS - 1).astype(jnp.int32)
    proj_value = centred(seeds[3], (PIECES, ATOM_SLOTS, PROJ, PTS), 0.2, 1.2, ((0, 64),), jnp.float32)
    kb_energy = jnp.clip(0.5 + 2.5 * jax.random.uniform(seeds[4], (ATOMS, PROJ), jnp.float32) ** block_levels(seeds[4], (ATOMS, PROJ), ((0, 64),), -0.2, 0.2), 0.5, 3.0)
    return {"psi_in": psi_in, "v_local": v_local, "proj_index": proj_index, "proj_value": proj_value, "kb_energy": kb_energy}


LAP_COEF = (-5369.0 / 1800.0, 12.0 / 7.0, -15.0 / 56.0, 10.0 / 189.0, -1.0 / 112.0, 2.0 / 1925.0, -1.0 / 16632.0)
HIGH = lax.Precision.HIGHEST


def laplace_full(field):
    result = 3.0 * LAP_COEF[0] * field
    for axis in (1, 2, 3):
        for offset in range(1, 7):
            result = result + LAP_COEF[offset] * (jnp.roll(field, offset, axis) + jnp.roll(field, -offset, axis))
    return result


def nonlocal_full(field, proj_index, proj_value, kb_energy):
    orbitals = field.shape[0]
    flattened = field.reshape(orbitals, -1)
    global_index = (jnp.arange(N_GRID, dtype=jnp.int32) * CELLS)[:, None, None, None] + proj_index.reshape(N_GRID, 3, ATOM_SLOTS, PTS).astype(jnp.int32)
    columns = global_index.reshape(-1)
    values = proj_value.reshape(N_GRID, 3, ATOM_SLOTS, PROJ, PTS)
    picked = flattened[:, columns].reshape(orbitals, N_GRID, 3, ATOM_SLOTS, PTS)
    partial_value = jnp.einsum('gkamp,ogkap->gkamo', values, picked, precision=HIGH)
    summed = partial_value[:, 1] + jnp.roll(partial_value[:, 2], 1, 0) + jnp.roll(partial_value[:, 0], -1, 0)
    scaled = summed * kb_energy.reshape(N_GRID, ATOM_SLOTS, PROJ)[..., None]
    returned = jnp.stack([jnp.roll(scaled, 1, 0), scaled, jnp.roll(scaled, -1, 0)], axis=1)
    contrib = jnp.einsum('gkamp,gkamo->ogkap', values, returned, precision=HIGH)
    result = jnp.zeros_like(flattened).at[:, columns].add(contrib.reshape(orbitals, -1))
    return result.reshape(field.shape)


def reference(psi_in, v_local, proj_index, proj_value, kb_energy):
    half_width = 6.0
    centre = 8.0
    sigma = half_width / (-3.0 - centre)
    sigma_two = 1.0 / (2.0 / sigma - sigma)

    def hamilton(field):
        return -0.5 * laplace_full(field) + v_local[None] * field + nonlocal_full(field, proj_index, proj_value, kb_energy)

    def filter_block(block):
        first = (hamilton(block) - centre * block) * (sigma / half_width)
        return (hamilton(first) - centre * first) * (2.0 * sigma_two / half_width) - (sigma * sigma_two) * block

    blocks = psi_in.reshape(NORB // 16, 16, NZ, NY, NX)
    filtered = lax.map(filter_block, blocks).reshape(NORB, NZ, NY, NX)
    flattened = filtered.reshape(NORB, -1)
    gram = jnp.dot(flattened, flattened.T, precision=HIGH, preferred_element_type=jnp.float32) / (NX * NY * NZ)
    return filtered, gram
```

```python
import functools

import jax
import jax.numpy as jnp
from jax import lax
from jax.experimental import pallas as pl
from jax.experimental.pallas import tpu as pltpu
from jax.sharding import PartitionSpec as P

LAP_COEF = (
    -5369.0 / 1800.0,
    12.0 / 7.0,
    -15.0 / 56.0,
    10.0 / 189.0,
    -1.0 / 112.0,
    2.0 / 1925.0,
    -1.0 / 16632.0,
)
HALF_WIDTH = 6.0
CENTRE = 8.0
SIGMA = HALF_WIDTH / (-3.0 - CENTRE)
SIGMA_TWO = 1.0 / (2.0 / SIGMA - SIGMA)

NX = 128
NY = 8
PLANES = 6
ROWS = PLANES * NY
SLOTS = 4
PROJ = 4
OWNED = SLOTS * PROJ
KAM = 3 * OWNED
PTS = 128

F32 = jnp.float32
BF16 = jnp.bfloat16
VMEM = pl.BlockSpec(memory_space=pltpu.VMEM)
SMEM = pl.BlockSpec(memory_space=pltpu.SMEM)


def two_parts(x):
    head = x.astype(BF16)
    return head, (x - head.astype(F32)).astype(BF16)


def dot_nt(lhs, rhs):
    return lax.dot_general(lhs, rhs, (((1,), (1,)), ((), ())), preferred_element_type=F32)


def dot_nn(lhs, rhs):
    return lax.dot_general(lhs, rhs, (((1,), (0,)), ((), ())), preferred_element_type=F32)


def row_of(field_ref, row, orbitals):
    return field_ref[pl.ds(row, orbitals, stride=ROWS), :]


def project(field_ref, proj_ref, orbitals):
    def step(pair, acc):
        row = 2 * pair
        points = jnp.concatenate([row_of(field_ref, row + i, orbitals) for i in (0, 1)], axis=1)
        head, tail = two_parts(points)
        lhs = jnp.concatenate([head, tail], axis=0)
        rhs = jnp.concatenate([proj_ref[row + i, : 2 * KAM, :] for i in (0, 1)], axis=1)
        return acc + dot_nt(lhs, rhs)

    acc = lax.fori_loop(0, ROWS // 2, step, jnp.zeros((2 * orbitals, 2 * KAM), F32), unroll=4)
    acc = acc[:orbitals] + acc[orbitals:]
    return acc[:, :KAM] + acc[:, KAM:]


def projector_kernel(odd_ref, index_ref, value_ref, psi_ref, proj_ref, part_ref, lhs_ref, *, orbitals):
    even = 1 - odd_ref[0]
    slot = lax.broadcasted_iota(jnp.int32, (OWNED, PTS), 0) // PROJ
    lane_no = lax.broadcasted_iota(jnp.int32, (NX, PTS), 0)
    row_no = lax.broadcasted_iota(jnp.int32, (ROWS, OWNED, PTS), 0)
    for frame in range(3):
        piece = frame + even * (2 - 2 * frame)
        index = index_ref[piece]
        value = value_ref[piece]
        parts = [p.astype(F32) for p in two_parts(value)]
        hits = []
        for a in range(SLOTS):
            mine = index[a : a + 1, :]
            row = jnp.where(slot == a, jnp.broadcast_to(mine >> 7, (OWNED, PTS)), -1)
            here = row_no == row[None]
            for i, part in enumerate(parts):
                chosen = jnp.where(here, part[None], 0.0)
                lhs_ref[i, :, a * PTS : (a + 1) * PTS] = chosen.reshape(ROWS * OWNED, PTS).astype(BF16)
            hits.append(jnp.where(lane_no == jnp.broadcast_to(mine & (NX - 1), (NX, PTS)), 1.0, 0.0).astype(BF16))
        rhs = jnp.concatenate(hits, axis=1)
        dense = dot_nt(lhs_ref[0], rhs) + dot_nt(lhs_ref[1], rhs)
        head, tail = two_parts(dense.reshape(ROWS, OWNED, NX))
        at = frame * OWNED
        proj_ref[:, at : at + OWNED, :] = head
        proj_ref[:, KAM + at : KAM + at + OWNED, :] = tail
        proj_ref[:, 2 * KAM + at : 2 * KAM + at + OWNED, :] = head
    part_ref[...] = project(psi_ref, proj_ref, orbitals)


def hamilton_kernel(odd_ref, field_ref, mate_ref, far_ref, proj_ref, v_ref, coeff_ref, *rest, orbitals, scale, back):
    if back is None:
        out_ref, part_ref, nonlocal_ref, v_scr = rest
    else:
        start_ref, out_ref, rows_ref, nonlocal_ref, v_scr = rest
    odd = odd_ref[0]
    head, tail = two_parts(coeff_ref[...] * scale)
    lhs = jnp.concatenate([head, head, tail], axis=1)

    def spread(pair, carry):
        row = 2 * pair
        rhs = jnp.concatenate([proj_ref[row + i] for i in (0, 1)], axis=1)
        both = dot_nn(lhs, rhs)
        for i in (0, 1):
            nonlocal_ref[pl.ds(row + i, orbitals, stride=ROWS), :] = both[:, i * NX : (i + 1) * NX]
        return carry

    lax.fori_loop(0, ROWS // 2, spread, 0, unroll=4)
    v_scr[...] = (v_ref[...] - (CENTRE + 1.5 * LAP_COEF[0])) * scale

    c = [-0.5 * scale * x for x in LAP_COEF]
    place = [(NY * ((PLANES - 1 - j) + odd * (2 * j - PLANES + 1))) for j in range(PLANES)]

    def orbital(o, carry):
        base = o * ROWS
        spots = [pl.ds(pl.multiple_of(base + p, NY), NY) for p in place]
        cells = [ref[s, :] for ref in (mate_ref, field_ref, far_ref) for s in spots]
        for j in range(PLANES):
            f = cells[PLANES + j]
            total = f * v_scr[pl.ds(pl.multiple_of(place[j], NY), NY), :] + nonlocal_ref[spots[j], :]
            if back is not None:
                total = total + back * start_ref[spots[j], :]
            for k in range(1, 7):
                along = (cells[PLANES + j + k] + cells[PLANES + j - k]) + (
                    pltpu.roll(f, k, 1) + pltpu.roll(f, NX - k, 1)
                )
                total = total + c[k] * along
            for k, weight in ((1, c[1]), (2, c[2] + c[6]), (3, c[3] + c[5])):
                total = total + weight * (pltpu.roll(f, k, 0) + pltpu.roll(f, NY - k, 0))
            total = total + (2.0 * c[4]) * pltpu.roll(f, 4, 0)
            out_ref[spots[j], :] = total
        return carry

    lax.fori_loop(0, orbitals, orbital, 0)
    if back is None:
        part_ref[...] = project(out_ref, proj_ref, orbitals)
    else:
        for row in range(ROWS):
            rows_ref[row] = row_of(out_ref, row, orbitals)


def gram_kernel(rows_ref, out_ref, *, groups, rows, scale):
    acc = None
    for row in range(0, rows, 2):
        x = jnp.concatenate(
            [
                jnp.concatenate([rows_ref[g * rows + row + i] for g in range(groups)], axis=0)
                for i in (0, 1)
            ],
            axis=1,
        )
        head, tail = two_parts(x)
        term = dot_nt(jnp.concatenate([head, tail], axis=0), head)
        acc = term if acc is None else acc + term
    n = acc.shape[1]
    cross = acc[n:]
    out_ref[...] = (acc[:n] + cross + cross.T) * scale


def on_device(psi_in, v_local, proj_index, proj_value, kb_energy):
    orbitals = psi_in.shape[0]
    cells = ROWS * NX
    slabs = lax.axis_size("grid")
    groups = lax.axis_size("orb")
    mates = [(i, i ^ 1) for i in range(slabs)]
    fars = [(i, (i + 1 if i % 2 else i - 1) % slabs) for i in range(slabs)]

    def swap(x, pairs):
        return lax.ppermute(x, "grid", pairs)

    odd = (lax.axis_index("grid") % 2).astype(jnp.int32).reshape(1)
    field_shape = jax.ShapeDtypeStruct((orbitals * ROWS, NX), F32)
    part_shape = jax.ShapeDtypeStruct((orbitals, KAM), F32)
    psi = psi_in.reshape(orbitals * ROWS, NX)
    v = v_local.reshape(ROWS, NX)
    kb = jnp.broadcast_to(kb_energy.reshape(1, OWNED), (orbitals, OWNED))

    def atoms(part):
        mate = swap(part[:, :OWNED], mates)
        own = part[:, OWNED : 2 * OWNED] + mate
        far = swap(jnp.concatenate([part[:, 2 * OWNED :], own, kb], axis=1), fars)
        own = (own + far[:, :OWNED]) * kb
        beyond = (far[:, OWNED : 2 * OWNED] + part[:, 2 * OWNED :]) * far[:, 2 * OWNED :]
        return jnp.concatenate([swap(own, mates), own, beyond], axis=1)

    def hamilton(field, mate, far, proj, coeff, scale, back, *start):
        second = part_shape if back is None else jax.ShapeDtypeStruct((ROWS, orbitals, NX), F32)
        return pl.pallas_call(
            functools.partial(hamilton_kernel, orbitals=orbitals, scale=scale, back=back),
            out_shape=(field_shape, second),
            in_specs=[SMEM] + [VMEM] * (6 + len(start)),
            out_specs=(VMEM, VMEM),
            scratch_shapes=[pltpu.VMEM((orbitals * ROWS, NX), F32), pltpu.VMEM((ROWS, NX), F32)],
            cost_estimate=pl.CostEstimate(flops=10**8, bytes_accessed=6 * 10**6, transcendentals=0),
            name="hamilton",
        )(odd, field, mate, far, proj, v, coeff, *start)

    psi_far = swap(psi, fars)
    psi_mate = swap(psi, mates)
    proj, part = pl.pallas_call(
        functools.partial(projector_kernel, orbitals=orbitals),
        out_shape=(jax.ShapeDtypeStruct((ROWS, 3 * KAM, NX), BF16), part_shape),
        in_specs=[SMEM] + [VMEM] * 3,
        out_specs=(VMEM, VMEM),
        scratch_shapes=[pltpu.VMEM((2, ROWS * OWNED, SLOTS * PTS), BF16)],
        cost_estimate=pl.CostEstimate(flops=10**8, bytes_accessed=3 * 10**6, transcendentals=0),
        name="projectors",
    )(odd, proj_index, proj_value.reshape(3, OWNED, PTS), psi)
    coeff = atoms(part)
    first, part = hamilton(psi, psi_mate, psi_far, proj, coeff, SIGMA / HALF_WIDTH, None)
    first_far = swap(first, fars)
    first_mate = swap(first, mates)
    coeff = atoms(part)
    filtered, rows = hamilton(
        first, first_mate, first_far, proj, coeff, 2.0 * SIGMA_TWO / HALF_WIDTH, -SIGMA * SIGMA_TWO, psi
    )
    rows = lax.all_to_all(rows, "orb", 0, 0, tiled=True)
    n = orbitals * groups
    partial_gram = pl.pallas_call(
        functools.partial(gram_kernel, groups=groups, rows=ROWS // groups, scale=1.0 / (cells * slabs)),
        out_shape=jax.ShapeDtypeStruct((n, n), F32),
        in_specs=[VMEM],
        out_specs=VMEM,
        cost_estimate=pl.CostEstimate(flops=10**8, bytes_accessed=10**6, transcendentals=0),
        name="gram",
    )(rows)
    width = n // slabs
    tiles = partial_gram.reshape(slabs, width, groups, orbitals).transpose(0, 2, 1, 3)
    tiles = lax.all_to_all(
        tiles.reshape(slabs * groups, width * orbitals), ("grid", "orb"), 0, 0, tiled=True
    )
    gram = jnp.sum(tiles, axis=0).reshape(width, orbitals).T
    return filtered.reshape(psi_in.shape), gram


def solution(mesh):
    placed = (
        P("orb", "grid", None, None),
        P("grid", None, None),
        P("grid", None, None),
        P("grid", None, None, None),
        P("grid", None),
    )
    return jax.shard_map(
        on_device,
        mesh=mesh,
        in_specs=placed,
        out_specs=(P("orb", "grid", None, None), P("orb", "grid")),
        check_vma=False,
    )
```

```python
import functools

import jax
import jax.numpy as jnp
from jax import lax
from jax.experimental import pallas as pl
from jax.experimental.pallas import tpu as pltpu
from jax.sharding import PartitionSpec as P

LAP_COEF = (
    -5369.0 / 1800.0,
    12.0 / 7.0,
    -15.0 / 56.0,
    10.0 / 189.0,
    -1.0 / 112.0,
    2.0 / 1925.0,
    -1.0 / 16632.0,
)
HALF_WIDTH = 6.0
CENTRE = 8.0
SIGMA = HALF_WIDTH / (-3.0 - CENTRE)
SIGMA_TWO = 1.0 / (2.0 / SIGMA - SIGMA)

NX = 128
NY = 8
PLANES = 6
ROWS = PLANES * NY
SLOTS = 4
PROJ = 4
OWNED = SLOTS * PROJ
KAM = 3 * OWNED
PTS = 128

F32 = jnp.float32
BF16 = jnp.bfloat16
VMEM = pl.BlockSpec(memory_space=pltpu.VMEM)
SMEM = pl.BlockSpec(memory_space=pltpu.SMEM)


def two_parts(x):
    head = x.astype(BF16)
    return head, (x - head.astype(F32)).astype(BF16)


def dot_nt(lhs, rhs):
    return lax.dot_general(lhs, rhs, (((1,), (1,)), ((), ())), preferred_element_type=F32)


def dot_nn(lhs, rhs):
    return lax.dot_general(lhs, rhs, (((1,), (0,)), ((), ())), preferred_element_type=F32)


def row_of(field_ref, row, orbitals):
    return field_ref[pl.ds(row, orbitals, stride=ROWS), :]


def lanes(shape):
    return lax.broadcasted_iota(jnp.int32, shape, 1)


def project(field_ref, proj_ref, orbitals):
    def step(pair, acc):
        row = 2 * pair
        points = jnp.concatenate([row_of(field_ref, row + i, orbitals) for i in (0, 1)], axis=1)
        head, tail = two_parts(points)
        lhs = jnp.concatenate([head, tail], axis=0)
        rhs = jnp.concatenate([proj_ref[row + i, :NX, :] for i in (0, 1)], axis=1)
        return acc + dot_nt(lhs, rhs)

    acc = lax.fori_loop(0, ROWS // 2, step, jnp.zeros((2 * orbitals, NX), F32), unroll=4)
    acc = acc[:orbitals] + acc[orbitals:]
    return jnp.where(lanes(acc.shape) < KAM, acc + pltpu.roll(acc, NX - KAM, 1), 0.0)


def put_messages(part, kb_ref, own_ref, mate_ref):
    lane = lanes(part.shape)
    kb = jnp.broadcast_to(kb_ref[...], part.shape)
    own_ref[...] = jnp.where(lane < KAM, part, jnp.where(lane < KAM + OWNED, kb, 0.0))
    mate = jnp.where(lane < 4 * OWNED, pltpu.roll(part, 3 * OWNED, 1), kb)
    mate = jnp.where(lane < 2 * OWNED, pltpu.roll(part, OWNED, 1), mate)
    mate = jnp.where(lane < 5 * OWNED, jnp.where(lane < 4 * OWNED, mate, pltpu.roll(part, 3 * OWNED, 1)), kb)
    sent = ((lane >= OWNED) & (lane < 2 * OWNED)) | ((lane >= 4 * OWNED) & (lane < 6 * OWNED))
    mate_ref[...] = jnp.where(sent, mate, 0.0)


def projector_kernel(odd_ref, index_ref, value_ref, kb_ref, psi_ref, proj_ref, own_ref, mate_ref, lhs_ref, *, orbitals):
    even = 1 - odd_ref[0]
    slot = lax.broadcasted_iota(jnp.int32, (OWNED, PTS), 0) // PROJ
    lane_no = lax.broadcasted_iota(jnp.int32, (NX, PTS), 0)
    row_no = lax.broadcasted_iota(jnp.int32, (ROWS, OWNED, PTS), 0)
    for frame in range(3):
        piece = frame + even * (2 - 2 * frame)
        index = index_ref[piece]
        value = value_ref[piece]
        parts = [p.astype(F32) for p in two_parts(value)]
        hits = []
        for a in range(SLOTS):
            mine = index[a : a + 1, :]
            row = jnp.where(slot == a, jnp.broadcast_to(mine >> 7, (OWNED, PTS)), -1)
            here = row_no == row[None]
            for i, part in enumerate(parts):
                chosen = jnp.where(here, part[None], 0.0)
                lhs_ref[i, :, a * PTS : (a + 1) * PTS] = chosen.reshape(ROWS * OWNED, PTS).astype(BF16)
            hits.append(jnp.where(lane_no == jnp.broadcast_to(mine & (NX - 1), (NX, PTS)), 1.0, 0.0).astype(BF16))
        rhs = jnp.concatenate(hits, axis=1)
        dense = dot_nt(lhs_ref[0], rhs) + dot_nt(lhs_ref[1], rhs)
        head, tail = two_parts(dense.reshape(ROWS, OWNED, NX))
        at = frame * OWNED
        proj_ref[:, at : at + OWNED, :] = head
        proj_ref[:, KAM + at : KAM + at + OWNED, :] = tail
        proj_ref[:, 2 * KAM + at : 2 * KAM + at + OWNED, :] = head
    put_messages(project(psi_ref, proj_ref, orbitals), kb_ref, own_ref, mate_ref)


def weights(scale):
    return [-0.5 * scale * x for x in LAP_COEF]


def places(odd_ref):
    odd = odd_ref[0]
    return [NY * ((PLANES - 1 - j) + odd * (2 * j - PLANES + 1)) for j in range(PLANES)]


def slab_kernel(field_ref, v_ref, *rest, orbitals, scale, back):
    start_ref = rest[0] if back is not None else None
    out_ref, v_scr = rest[-2:]
    v_scr[...] = (v_ref[...] - (CENTRE + 1.5 * LAP_COEF[0])) * scale
    c = weights(scale)

    def orbital(o, carry):
        base = o * ROWS
        spots = [pl.ds(pl.multiple_of(base + NY * j, NY), NY) for j in range(PLANES)]
        cells = [field_ref[s, :] for s in spots]
        for j in range(PLANES):
            f = cells[j]
            total = f * v_scr[NY * j : NY * j + NY, :]
            if back is not None:
                total = total + back * start_ref[spots[j], :]
            for k in range(1, 7):
                along = pltpu.roll(f, k, 1) + pltpu.roll(f, NX - k, 1)
                for other in (j - k, j + k):
                    if 0 <= other < PLANES:
                        along = along + cells[other]
                total = total + c[k] * along
            for k, weight in ((1, c[1]), (2, c[2] + c[6]), (3, c[3] + c[5])):
                total = total + weight * (pltpu.roll(f, k, 0) + pltpu.roll(f, NY - k, 0))
            total = total + (2.0 * c[4]) * pltpu.roll(f, 4, 0)
            out_ref[spots[j], :] = total
        return carry

    lax.fori_loop(0, orbitals, orbital, 0)


def finish_kernel(place_ref, slab_ref, mate_ref, far_ref, proj_ref, own_msg, far_msg, beyond_msg, *rest, orbitals, scale, last):
    if last:
        out_ref, *chunk_refs, nonlocal_ref = rest
    else:
        kb_ref, out_ref, own_out, mate_out, nonlocal_ref = rest
    own, far, beyond = own_msg[...], far_msg[...], beyond_msg[...]
    lane = lanes(own.shape)

    def shift(x, by):
        return pltpu.roll(x, NX - by, 1)

    first, second = lane < OWNED, lane < 2 * OWNED
    sums = own + jnp.where(
        first,
        shift(own, 4 * OWNED) + shift(beyond, 2 * OWNED),
        jnp.where(second, shift(far, OWNED), pltpu.roll(far, OWNED, 1)),
    )
    energy = jnp.where(
        first, shift(own, 5 * OWNED), jnp.where(second, shift(own, 2 * OWNED), shift(far, OWNED))
    )
    coeff = (sums * energy * scale)[:, :KAM]
    head, tail = two_parts(coeff)
    lhs = jnp.concatenate([head, head, tail], axis=1)

    def spread(pair, carry):
        row = 2 * pair
        rhs = jnp.concatenate([proj_ref[row + i] for i in (0, 1)], axis=1)
        both = dot_nn(lhs, rhs)
        for i in (0, 1):
            nonlocal_ref[pl.ds(row + i, orbitals, stride=ROWS), :] = both[:, i * NX : (i + 1) * NX]
        return carry

    lax.fori_loop(0, ROWS // 2, spread, 0, unroll=4)
    c = weights(scale)
    place = places(place_ref)

    def orbital(o, carry):
        base = o * ROWS
        spots = [pl.ds(pl.multiple_of(base + p, NY), NY) for p in place]
        mate = [mate_ref[s, :] for s in spots]
        beyond = [far_ref[s, :] for s in spots]
        for j in range(PLANES):
            total = slab_ref[spots[j], :] + nonlocal_ref[spots[j], :]
            for k in range(1, 7):
                terms = []
                if j - k < 0:
                    terms.append(mate[PLANES + j - k])
                if j + k >= PLANES:
                    terms.append(beyond[j + k - PLANES])
                if terms:
                    total = total + c[k] * sum(terms[1:], terms[0])
            out_ref[spots[j], :] = total
        return carry

    lax.fori_loop(0, orbitals, orbital, 0, unroll=2)
    if last:
        share = ROWS // len(chunk_refs)
        for m, chunk_ref in enumerate(chunk_refs):
            at = (place_ref[1] ^ m) * share
            for i in range(share):
                chunk_ref[i] = row_of(out_ref, at + i, orbitals)
    else:
        put_messages(project(out_ref, proj_ref, orbitals), kb_ref, own_out, mate_out)


def gram_kernel(place_ref, *refs, orbitals, width, scale):
    *block_refs, out_ref, head_ref, tail_ref, gram_ref = refs
    for m, block_ref in enumerate(block_refs):
        at = pl.ds(pl.multiple_of((place_ref[1] ^ m) * orbitals, orbitals), orbitals)
        for i in range(block_ref.shape[0]):
            head, tail = two_parts(block_ref[i])
            head_ref[at, i * NX : (i + 1) * NX] = head
            tail_ref[at, i * NX : (i + 1) * NX] = tail
    head = head_ref[...]
    cross = dot_nt(tail_ref[...], head)
    gram_ref[...] = (dot_nt(head, head) + cross + cross.T) * scale
    n = gram_ref.shape[0]
    groups = len(block_refs)
    parts = [gram_ref[pl.ds(t, n // width, stride=width), :] for t in range(width)]
    lane = lanes(parts[0].shape)
    for q in range(groups):
        row = parts[0] if q == 0 else pltpu.roll(parts[0], n - orbitals * q, 1)
        for t in range(1, width):
            by = (orbitals * (t - q)) % n
            row = jnp.where(lane < orbitals * t, row, pltpu.roll(parts[t], by, 1) if by else parts[t])
        out_ref[pl.ds(q, n // width, stride=groups), :] = row


def params(mib):
    return pltpu.CompilerParams(vmem_limit_bytes=mib * 2**20)


def on_device(psi_in, v_local, proj_index, proj_value, kb_energy):
    orbitals = psi_in.shape[0]
    slabs = lax.axis_size("grid")
    groups = lax.axis_size("orb")
    mates = [(i, i ^ 1) for i in range(slabs)]
    fars = [(i, (i + 1 if i % 2 else i - 1) % slabs) for i in range(slabs)]
    n = orbitals * groups
    width = n // slabs

    def swap(x, pairs):
        return lax.ppermute(x, "grid", pairs)

    place = jnp.stack([lax.axis_index("grid") % 2, lax.axis_index("orb")]).astype(jnp.int32)
    field_shape = jax.ShapeDtypeStruct((orbitals * ROWS, NX), F32)
    message_shape = jax.ShapeDtypeStruct((orbitals, NX), F32)
    psi = psi_in.reshape(orbitals * ROWS, NX)
    v = v_local.reshape(ROWS, NX)
    kb = kb_energy.reshape(1, OWNED)
    kb = jnp.pad(kb, ((0, 0), (KAM, 0))) + jnp.zeros((1, KAM + OWNED), F32)
    kb = jnp.pad(jnp.concatenate([kb, kb[:, 2 * OWNED :]], axis=1), ((0, 0), (0, NX - 6 * OWNED)))

    def slab(field, scale, back, *start):
        return pl.pallas_call(
            functools.partial(slab_kernel, orbitals=orbitals, scale=scale, back=back),
            out_shape=field_shape,
            in_specs=[VMEM] * (2 + len(start)),
            out_specs=VMEM,
            scratch_shapes=[pltpu.VMEM((ROWS, NX), F32)],
            compiler_params=params(8),
            cost_estimate=pl.CostEstimate(flops=10**8, bytes_accessed=10**7, transcendentals=0),
            name="slab",
        )(field, v, *start)

    def finish(operands, outs, scale, last):
        return pl.pallas_call(
            functools.partial(finish_kernel, orbitals=orbitals, scale=scale, last=last),
            out_shape=(field_shape, *outs),
            in_specs=[SMEM] + [VMEM] * len(operands),
            out_specs=(VMEM,) * (1 + len(outs)),
            scratch_shapes=[pltpu.VMEM((orbitals * ROWS, NX), F32)],
            compiler_params=params(16),
            cost_estimate=pl.CostEstimate(flops=10**8, bytes_accessed=10**7, transcendentals=0),
            name="finish",
        )(place, *operands)

    def stage(field, proj, own, to_mate, scale, back, *start):
        far = swap(field, fars)
        mate = swap(field, mates)
        own = own + swap(to_mate, mates)
        from_far = swap(own, fars)
        field, own = lax.optimization_barrier((field, own))
        local = slab(field, scale, back, *start)
        return local, mate, far, proj, own, from_far, swap(from_far, mates)

    proj, own, to_mate = pl.pallas_call(
        functools.partial(projector_kernel, orbitals=orbitals),
        out_shape=(jax.ShapeDtypeStruct((ROWS, 3 * KAM, NX), BF16), message_shape, message_shape),
        in_specs=[SMEM] + [VMEM] * 4,
        out_specs=(VMEM,) * 3,
        scratch_shapes=[pltpu.VMEM((2, ROWS * OWNED, SLOTS * PTS), BF16)],
        compiler_params=params(16),
        cost_estimate=pl.CostEstimate(flops=10**8, bytes_accessed=10**7, transcendentals=0),
        name="projectors",
    )(place, proj_index, proj_value.reshape(3, OWNED, PTS), kb, psi)
    scale = SIGMA / HALF_WIDTH
    operands = stage(psi, proj, own, to_mate, scale, None)
    first, own, to_mate = finish((*operands, kb), (message_shape,) * 2, scale, False)
    scale = 2.0 * SIGMA_TWO / HALF_WIDTH
    operands = stage(first, proj, own, to_mate, scale, -SIGMA * SIGMA_TWO, psi)
    chunk = jax.ShapeDtypeStruct((ROWS // groups, orbitals, NX), F32)
    filtered, *blocks = finish(operands, (chunk,) * groups, scale, True)
    for m in reversed(range(1, groups)):
        blocks[m] = lax.ppermute(blocks[m], "orb", [(i, i ^ m) for i in range(groups)])
    tiles = pl.pallas_call(
        functools.partial(gram_kernel, orbitals=orbitals, width=width, scale=1.0 / (slabs * ROWS * NX)),
        out_shape=jax.ShapeDtypeStruct((slabs * groups, n), F32),
        in_specs=[SMEM] + [VMEM] * groups,
        out_specs=VMEM,
        scratch_shapes=[pltpu.VMEM((n, ROWS // groups * NX), BF16)] * 2 + [pltpu.VMEM((n, n), F32)],
        compiler_params=params(8),
        cost_estimate=pl.CostEstimate(flops=10**8, bytes_accessed=10**6, transcendentals=0),
        name="gram",
    )(place, *blocks)
    tiles = lax.all_to_all(tiles, ("grid", "orb"), 0, 0, tiled=True)
    gram = jnp.sum(tiles, axis=0)[: width * orbitals].reshape(width, orbitals).T
    return filtered.reshape(psi_in.shape), gram


def solution(mesh):
    placed = (
        P("orb", "grid", None, None),
        P("grid", None, None),
        P("grid", None, None),
        P("grid", None, None, None),
        P("grid", None),
    )
    return jax.shard_map(
        on_device,
        mesh=mesh,
        in_specs=placed,
        out_specs=(P("orb", "grid", None, None), P("orb", "grid")),
        check_vma=False,
    )
```

```python
import functools

import jax
import jax.numpy as jnp
from jax import lax
from jax.experimental import pallas as pl
from jax.experimental.pallas import tpu as pltpu
from jax.sharding import PartitionSpec as P

LAP_COEF = (
    -5369.0 / 1800.0,
    12.0 / 7.0,
    -15.0 / 56.0,
    10.0 / 189.0,
    -1.0 / 112.0,
    2.0 / 1925.0,
    -1.0 / 16632.0,
)
HALF_WIDTH = 6.0
CENTRE = 8.0
SIGMA = HALF_WIDTH / (-3.0 - CENTRE)
SIGMA_TWO = 1.0 / (2.0 / SIGMA - SIGMA)

NX = 128
NY = 8
PLANES = 6
ROWS = PLANES * NY
SLOTS = 4
PROJ = 4
OWNED = SLOTS * PROJ
KAM = 3 * OWNED
PTS = 128

F32 = jnp.float32
BF16 = jnp.bfloat16
VMEM = pl.BlockSpec(memory_space=pltpu.VMEM)
SMEM = pl.BlockSpec(memory_space=pltpu.SMEM)


def two_parts(x):
    head = x.astype(BF16)
    return head, (x - head.astype(F32)).astype(BF16)


def dot_nt(lhs, rhs):
    return lax.dot_general(lhs, rhs, (((1,), (1,)), ((), ())), preferred_element_type=F32)


def dot_nn(lhs, rhs):
    return lax.dot_general(lhs, rhs, (((1,), (0,)), ((), ())), preferred_element_type=F32)


def row_of(field_ref, row, orbitals):
    return field_ref[pl.ds(row, orbitals, stride=ROWS), :]


def lanes(shape):
    return lax.broadcasted_iota(jnp.int32, shape, 1)


def project(field_ref, proj_ref, orbitals):
    def step(pair, acc):
        row = 2 * pair
        points = jnp.concatenate([row_of(field_ref, row + i, orbitals) for i in (0, 1)], axis=1)
        head, tail = two_parts(points)
        lhs = jnp.concatenate([head, tail], axis=0)
        rhs = jnp.concatenate([proj_ref[row + i, :NX, :] for i in (0, 1)], axis=1)
        return acc + dot_nt(lhs, rhs)

    acc = lax.fori_loop(0, ROWS // 2, step, jnp.zeros((2 * orbitals, NX), F32), unroll=4)
    acc = acc[:orbitals] + acc[orbitals:]
    return jnp.where(lanes(acc.shape) < KAM, acc + pltpu.roll(acc, NX - KAM, 1), 0.0)


def put_messages(part, kb_ref, own_ref, mate_ref):
    lane = lanes(part.shape)
    kb = jnp.broadcast_to(kb_ref[...], part.shape)
    own_ref[...] = jnp.where(lane < KAM, part, jnp.where(lane < KAM + OWNED, kb, 0.0))
    mate = jnp.where(lane < 4 * OWNED, pltpu.roll(part, 3 * OWNED, 1), kb)
    mate = jnp.where(lane < 2 * OWNED, pltpu.roll(part, OWNED, 1), mate)
    mate = jnp.where(lane < 5 * OWNED, jnp.where(lane < 4 * OWNED, mate, pltpu.roll(part, 3 * OWNED, 1)), kb)
    sent = ((lane >= OWNED) & (lane < 2 * OWNED)) | ((lane >= 4 * OWNED) & (lane < 6 * OWNED))
    mate_ref[...] = jnp.where(sent, mate, 0.0)


def projector_kernel(odd_ref, index_ref, value_ref, kb_ref, psi_ref, proj_ref, own_ref, mate_ref, lhs_ref, *, orbitals):
    even = 1 - odd_ref[0]
    slot = lax.broadcasted_iota(jnp.int32, (OWNED, PTS), 0) // PROJ
    lane_no = lax.broadcasted_iota(jnp.int32, (NX, PTS), 0)
    row_no = lax.broadcasted_iota(jnp.int32, (ROWS, OWNED, PTS), 0)
    for frame in range(3):
        piece = frame + even * (2 - 2 * frame)
        index = index_ref[piece]
        value = jnp.concatenate([value_ref[piece, a] for a in range(SLOTS)], axis=0)
        parts = [p.astype(F32) for p in two_parts(value)]
        hits = []
        for a in range(SLOTS):
            mine = index[a : a + 1, :]
            row = jnp.where(slot == a, jnp.broadcast_to(mine >> 7, (OWNED, PTS)), -1)
            here = row_no == row[None]
            for i, part in enumerate(parts):
                chosen = jnp.where(here, part[None], 0.0)
                lhs_ref[i, :, a * PTS : (a + 1) * PTS] = chosen.reshape(ROWS * OWNED, PTS).astype(BF16)
            hits.append(jnp.where(lane_no == jnp.broadcast_to(mine & (NX - 1), (NX, PTS)), 1.0, 0.0).astype(BF16))
        rhs = jnp.concatenate(hits, axis=1)
        dense = dot_nt(lhs_ref[0], rhs) + dot_nt(lhs_ref[1], rhs)
        head, tail = two_parts(dense.reshape(ROWS, OWNED, NX))
        at = frame * OWNED
        proj_ref[:, at : at + OWNED, :] = head
        proj_ref[:, KAM + at : KAM + at + OWNED, :] = tail
        proj_ref[:, 2 * KAM + at : 2 * KAM + at + OWNED, :] = head
    put_messages(project(psi_ref, proj_ref, orbitals), kb_ref, own_ref, mate_ref)


def weights(scale):
    return [-0.5 * scale * x for x in LAP_COEF]


def places(odd_ref):
    odd = odd_ref[0]
    return [NY * ((PLANES - 1 - j) + odd * (2 * j - PLANES + 1)) for j in range(PLANES)]


def slab_kernel(field_ref, v_ref, *rest, orbitals, scale, back):
    start_ref = rest[0] if back is not None else None
    out_ref, v_scr = rest[-2:]
    v_scr[...] = (v_ref[...] - (CENTRE + 1.5 * LAP_COEF[0])) * scale
    c = weights(scale)

    def orbital(o, carry):
        base = o * ROWS
        spots = [pl.ds(pl.multiple_of(base + NY * j, NY), NY) for j in range(PLANES)]
        cells = [field_ref[s, :] for s in spots]
        for j in range(PLANES):
            f = cells[j]
            total = f * v_scr[NY * j : NY * j + NY, :]
            if back is not None:
                total = total + back * start_ref[spots[j], :]
            for k in range(1, 7):
                along = pltpu.roll(f, k, 1) + pltpu.roll(f, NX - k, 1)
                for other in (j - k, j + k):
                    if 0 <= other < PLANES:
                        along = along + cells[other]
                total = total + c[k] * along
            for k, weight in ((1, c[1]), (2, c[2] + c[6]), (3, c[3] + c[5])):
                total = total + weight * (pltpu.roll(f, k, 0) + pltpu.roll(f, NY - k, 0))
            total = total + (2.0 * c[4]) * pltpu.roll(f, 4, 0)
            out_ref[spots[j], :] = total
        return carry

    lax.fori_loop(0, orbitals, orbital, 0)


def finish_kernel(place_ref, slab_ref, mate_ref, far_ref, proj_ref, own_msg, far_msg, beyond_msg, *rest, orbitals, scale, last):
    if last:
        out_ref, *chunk_refs, nonlocal_ref = rest
    else:
        kb_ref, out_ref, own_out, mate_out, nonlocal_ref = rest
    own, far, beyond = own_msg[...], far_msg[...], beyond_msg[...]
    lane = lanes(own.shape)

    def shift(x, by):
        return pltpu.roll(x, NX - by, 1)

    first, second = lane < OWNED, lane < 2 * OWNED
    sums = own + jnp.where(
        first,
        shift(own, 4 * OWNED) + shift(beyond, 2 * OWNED),
        jnp.where(second, shift(far, OWNED), pltpu.roll(far, OWNED, 1)),
    )
    energy = jnp.where(
        first, shift(own, 5 * OWNED), jnp.where(second, shift(own, 2 * OWNED), shift(far, OWNED))
    )
    coeff = (sums * energy * scale)[:, :KAM]
    head, tail = two_parts(coeff)
    lhs = jnp.concatenate([head, head, tail], axis=1)

    def spread(pair, carry):
        row = 2 * pair
        rhs = jnp.concatenate([proj_ref[row + i] for i in (0, 1)], axis=1)
        both = dot_nn(lhs, rhs)
        for i in (0, 1):
            nonlocal_ref[pl.ds(row + i, orbitals, stride=ROWS), :] = both[:, i * NX : (i + 1) * NX]
        return carry

    lax.fori_loop(0, ROWS // 2, spread, 0, unroll=4)
    c = weights(scale)
    place = places(place_ref)

    def orbital(o, carry):
        base = o * ROWS
        spots = [pl.ds(pl.multiple_of(base + p, NY), NY) for p in place]
        mate = [mate_ref[s, :] for s in spots]
        beyond = [far_ref[s, :] for s in spots]
        for j in range(PLANES):
            total = slab_ref[spots[j], :] + nonlocal_ref[spots[j], :]
            for k in range(1, 7):
                terms = []
                if j - k < 0:
                    terms.append(mate[PLANES + j - k])
                if j + k >= PLANES:
                    terms.append(beyond[j + k - PLANES])
                if terms:
                    total = total + c[k] * sum(terms[1:], terms[0])
            out_ref[spots[j], :] = total
        return carry

    lax.fori_loop(0, orbitals, orbital, 0, unroll=2)
    if last:
        share = ROWS // len(chunk_refs)
        for m, chunk_ref in enumerate(chunk_refs):
            at = (place_ref[1] ^ m) * share
            for i in range(share):
                chunk_ref[i] = row_of(out_ref, at + i, orbitals)
    else:
        put_messages(project(out_ref, proj_ref, orbitals), kb_ref, own_out, mate_out)


def gram_kernel(place_ref, *refs, orbitals, width, scale):
    *block_refs, out_ref, head_ref, tail_ref, gram_ref = refs
    for m, block_ref in enumerate(block_refs):
        at = pl.ds(pl.multiple_of((place_ref[1] ^ m) * orbitals, orbitals), orbitals)
        for i in range(block_ref.shape[0]):
            head, tail = two_parts(block_ref[i])
            head_ref[at, i * NX : (i + 1) * NX] = head
            tail_ref[at, i * NX : (i + 1) * NX] = tail
    head = head_ref[...]
    cross = dot_nt(tail_ref[...], head)
    gram_ref[...] = (dot_nt(head, head) + cross + cross.T) * scale
    n = gram_ref.shape[0]
    groups = len(block_refs)
    parts = [gram_ref[pl.ds(t, n // width, stride=width), :] for t in range(width)]
    lane = lanes(parts[0].shape)
    for q in range(groups):
        row = parts[0] if q == 0 else pltpu.roll(parts[0], n - orbitals * q, 1)
        for t in range(1, width):
            by = (orbitals * (t - q)) % n
            row = jnp.where(lane < orbitals * t, row, pltpu.roll(parts[t], by, 1) if by else parts[t])
        out_ref[pl.ds(q, n // width, stride=groups), :] = row


def params(mib):
    return pltpu.CompilerParams(vmem_limit_bytes=mib * 2**20)


def on_device(psi_in, v_local, proj_index, proj_value, kb_energy):
    orbitals = psi_in.shape[0]
    slabs = lax.axis_size("grid")
    groups = lax.axis_size("orb")
    mates = [(i, i ^ 1) for i in range(slabs)]
    fars = [(i, (i + 1 if i % 2 else i - 1) % slabs) for i in range(slabs)]
    n = orbitals * groups
    width = n // slabs

    def swap(x, pairs):
        return lax.ppermute(x, "grid", pairs)

    place = jnp.stack([lax.axis_index("grid") % 2, lax.axis_index("orb")]).astype(jnp.int32)
    field_shape = jax.ShapeDtypeStruct((orbitals * ROWS, NX), F32)
    message_shape = jax.ShapeDtypeStruct((orbitals, NX), F32)
    psi = psi_in.reshape(orbitals * ROWS, NX)
    v = v_local.reshape(ROWS, NX)
    kb = kb_energy.reshape(1, OWNED)
    kb = jnp.pad(kb, ((0, 0), (KAM, 0))) + jnp.zeros((1, KAM + OWNED), F32)
    kb = jnp.pad(jnp.concatenate([kb, kb[:, 2 * OWNED :]], axis=1), ((0, 0), (0, NX - 6 * OWNED)))

    def slab(field, scale, back, *start):
        return pl.pallas_call(
            functools.partial(slab_kernel, orbitals=orbitals, scale=scale, back=back),
            out_shape=field_shape,
            in_specs=[VMEM] * (2 + len(start)),
            out_specs=VMEM,
            scratch_shapes=[pltpu.VMEM((ROWS, NX), F32)],
            compiler_params=params(8),
            cost_estimate=pl.CostEstimate(flops=10**8, bytes_accessed=10**7, transcendentals=0),
            name="slab",
        )(field, v, *start)

    def finish(operands, outs, scale, last):
        return pl.pallas_call(
            functools.partial(finish_kernel, orbitals=orbitals, scale=scale, last=last),
            out_shape=(field_shape, *outs),
            in_specs=[SMEM] + [VMEM] * len(operands),
            out_specs=(VMEM,) * (1 + len(outs)),
            scratch_shapes=[pltpu.VMEM((orbitals * ROWS, NX), F32)],
            compiler_params=params(16),
            cost_estimate=pl.CostEstimate(flops=10**8, bytes_accessed=10**7, transcendentals=0),
            name="finish",
        )(place, *operands)

    def stage(field, proj, own, to_mate, scale, back, *start):
        far = swap(field, fars)
        mate = swap(field, mates)
        own = own + swap(to_mate, mates)
        from_far = swap(own, fars)
        field, own = lax.optimization_barrier((field, own))
        local = slab(field, scale, back, *start)
        from_far, local = lax.optimization_barrier((from_far, local))
        return local, mate, far, proj, own, from_far, swap(from_far, mates)

    proj, own, to_mate = pl.pallas_call(
        functools.partial(projector_kernel, orbitals=orbitals),
        out_shape=(jax.ShapeDtypeStruct((ROWS, 3 * KAM, NX), BF16), message_shape, message_shape),
        in_specs=[SMEM] + [VMEM] * 4,
        out_specs=(VMEM,) * 3,
        scratch_shapes=[pltpu.VMEM((2, ROWS * OWNED, SLOTS * PTS), BF16)],
        compiler_params=params(16),
        cost_estimate=pl.CostEstimate(flops=10**8, bytes_accessed=10**7, transcendentals=0),
        name="projectors",
    )(place, proj_index, proj_value, kb, psi)
    scale = SIGMA / HALF_WIDTH
    operands = stage(psi, proj, own, to_mate, scale, None)
    first, own, to_mate = finish((*operands, kb), (message_shape,) * 2, scale, False)
    scale = 2.0 * SIGMA_TWO / HALF_WIDTH
    operands = stage(first, proj, own, to_mate, scale, -SIGMA * SIGMA_TWO, psi)
    chunk = jax.ShapeDtypeStruct((ROWS // groups, orbitals, NX), F32)
    filtered, *blocks = finish(operands, (chunk,) * groups, scale, True)
    for m in reversed(range(1, groups)):
        blocks[m] = lax.ppermute(blocks[m], "orb", [(i, i ^ m) for i in range(groups)])
    tiles = pl.pallas_call(
        functools.partial(gram_kernel, orbitals=orbitals, width=width, scale=1.0 / (slabs * ROWS * NX)),
        out_shape=jax.ShapeDtypeStruct((slabs * groups, n), F32),
        in_specs=[SMEM] + [VMEM] * groups,
        out_specs=VMEM,
        scratch_shapes=[pltpu.VMEM((n, ROWS // groups * NX), BF16)] * 2 + [pltpu.VMEM((n, n), F32)],
        compiler_params=params(8),
        cost_estimate=pl.CostEstimate(flops=10**8, bytes_accessed=10**6, transcendentals=0),
        name="gram",
    )(place, *blocks)
    tiles = lax.all_to_all(tiles, ("grid", "orb"), 0, 0, tiled=True)
    gram = jnp.sum(tiles, axis=0)[: width * orbitals].reshape(width, orbitals).T
    return filtered.reshape(psi_in.shape), gram


def solution(mesh):
    placed = (
        P("orb", "grid", None, None),
        P("grid", None, None),
        P("grid", None, None),
        P("grid", None, None, None),
        P("grid", None),
    )
    return jax.shard_map(
        on_device,
        mesh=mesh,
        in_specs=placed,
        out_specs=(P("orb", "grid", None, None), P("orb", "grid")),
        check_vma=False,
    )
```

```python
import functools

import jax
import jax.numpy as jnp
from jax import lax
from jax.experimental import pallas as pl
from jax.experimental.pallas import tpu as pltpu
from jax.sharding import PartitionSpec as P

LAP_COEF = (
    -5369.0 / 1800.0,
    12.0 / 7.0,
    -15.0 / 56.0,
    10.0 / 189.0,
    -1.0 / 112.0,
    2.0 / 1925.0,
    -1.0 / 16632.0,
)
HALF_WIDTH = 6.0
CENTRE = 8.0
SIGMA = HALF_WIDTH / (-3.0 - CENTRE)
SIGMA_TWO = 1.0 / (2.0 / SIGMA - SIGMA)

NX = 128
NY = 8
PLANES = 6
ROWS = PLANES * NY
SLOTS = 4
PROJ = 4
OWNED = SLOTS * PROJ
KAM = 3 * OWNED
PTS = 128

F32 = jnp.float32
BF16 = jnp.bfloat16
VMEM = pl.BlockSpec(memory_space=pltpu.VMEM)
SMEM = pl.BlockSpec(memory_space=pltpu.SMEM)


def two_parts(x):
    head = x.astype(BF16)
    return head, (x - head.astype(F32)).astype(BF16)


def dot_nt(lhs, rhs):
    return lax.dot_general(lhs, rhs, (((1,), (1,)), ((), ())), preferred_element_type=F32)


def dot_nn(lhs, rhs):
    return lax.dot_general(lhs, rhs, (((1,), (0,)), ((), ())), preferred_element_type=F32)


def row_of(field_ref, row, orbitals):
    return field_ref[pl.ds(row, orbitals, stride=ROWS), :]


def lanes(shape):
    return lax.broadcasted_iota(jnp.int32, shape, 1)


def project(field_ref, proj_ref, orbitals):
    def step(pair, acc):
        row = 2 * pair
        points = jnp.concatenate([row_of(field_ref, row + i, orbitals) for i in (0, 1)], axis=1)
        head, tail = two_parts(points)
        lhs = jnp.concatenate([head, tail], axis=0)
        rhs = jnp.concatenate([proj_ref[row + i, :NX, :] for i in (0, 1)], axis=1)
        return acc + dot_nt(lhs, rhs)

    acc = lax.fori_loop(0, ROWS // 2, step, jnp.zeros((2 * orbitals, NX), F32), unroll=4)
    acc = acc[:orbitals] + acc[orbitals:]
    return jnp.where(lanes(acc.shape) < KAM, acc + pltpu.roll(acc, NX - KAM, 1), 0.0)


def put_messages(part, kb_ref, own_ref, mate_ref):
    lane = lanes(part.shape)
    kb = jnp.broadcast_to(kb_ref[...], part.shape)
    own_ref[...] = jnp.where(lane < KAM, part, jnp.where(lane < KAM + OWNED, kb, 0.0))
    mate = jnp.where(lane < 4 * OWNED, pltpu.roll(part, 3 * OWNED, 1), kb)
    mate = jnp.where(lane < 2 * OWNED, pltpu.roll(part, OWNED, 1), mate)
    mate = jnp.where(lane < 5 * OWNED, jnp.where(lane < 4 * OWNED, mate, pltpu.roll(part, 3 * OWNED, 1)), kb)
    sent = ((lane >= OWNED) & (lane < 2 * OWNED)) | ((lane >= 4 * OWNED) & (lane < 6 * OWNED))
    mate_ref[...] = jnp.where(sent, mate, 0.0)


def fill_projectors(even, index_of, value_of, proj_ref, lhs_ref):
    slot = lax.broadcasted_iota(jnp.int32, (OWNED, PTS), 0) // PROJ
    lane_no = lax.broadcasted_iota(jnp.int32, (NX, PTS), 0)
    row_no = lax.broadcasted_iota(jnp.int32, (ROWS, OWNED, PTS), 0)
    for frame in range(3):
        piece = frame + even * (2 - 2 * frame)
        index = index_of(piece)
        value = value_of(piece)
        parts = [p.astype(F32) for p in two_parts(value)]
        hits = []
        for a in range(SLOTS):
            mine = index[a : a + 1, :]
            row = jnp.where(slot == a, jnp.broadcast_to(mine >> 7, (OWNED, PTS)), -1)
            here = row_no == row[None]
            for i, part in enumerate(parts):
                chosen = jnp.where(here, part[None], 0.0)
                lhs_ref[i, :, a * PTS : (a + 1) * PTS] = chosen.reshape(ROWS * OWNED, PTS).astype(BF16)
            hits.append(jnp.where(lane_no == jnp.broadcast_to(mine & (NX - 1), (NX, PTS)), 1.0, 0.0).astype(BF16))
        rhs = jnp.concatenate(hits, axis=1)
        dense = dot_nt(lhs_ref[0], rhs) + dot_nt(lhs_ref[1], rhs)
        head, tail = two_parts(dense.reshape(ROWS, OWNED, NX))
        at = frame * OWNED
        proj_ref[:, at : at + OWNED, :] = head
        proj_ref[:, KAM + at : KAM + at + OWNED, :] = tail
        proj_ref[:, 2 * KAM + at : 2 * KAM + at + OWNED, :] = head


def projector_kernel(place_ref, index_ref, value_ref, kb_ref, psi_ref, proj_ref, own_ref, mate_ref, lhs_ref, *, orbitals):
    def value_of(piece):
        return jnp.concatenate([value_ref[piece, a] for a in range(SLOTS)], axis=0)

    fill_projectors(1 - place_ref[0], lambda piece: index_ref[piece], value_of, proj_ref, lhs_ref)
    put_messages(project(psi_ref, proj_ref, orbitals), kb_ref, own_ref, mate_ref)


def far_projector_kernel(place_ref, message_ref, proj_ref, lhs_ref, *, index_at, value_at):
    def index_of(piece):
        return message_ref[pl.ds(index_at + piece * SLOTS, SLOTS), :].astype(jnp.int32)

    def value_of(piece):
        return message_ref[pl.ds(pl.multiple_of(value_at + piece * OWNED, 8), OWNED), :]

    fill_projectors(place_ref[0], index_of, value_of, proj_ref, lhs_ref)


def weights(scale):
    return [-0.5 * scale * x for x in LAP_COEF]


def places(odd):
    return [NY * ((PLANES - 1 - j) + odd * (2 * j - PLANES + 1)) for j in range(PLANES)]


def banded(size, period, c):
    i, j = (lax.broadcasted_iota(jnp.int32, (size, size), d) for d in (0, 1))
    ahead = (j - i) & (period - 1)
    matrix = jnp.zeros((size, size), F32)
    for k in range(1, 7):
        for by in (k, -k):
            matrix = matrix + jnp.where(ahead == by % period, c[k], 0.0)
    return two_parts(jnp.where(i // period == j // period, matrix, 0.0))


def slab_kernel(field_ref, v_ref, *rest, orbitals, scale, back):
    start_ref = rest[0] if back is not None else None
    out_ref, v_scr, planar_ref = rest[-3:]
    v_scr[...] = (v_ref[...] - (CENTRE + 1.5 * LAP_COEF[0])) * scale
    c = weights(scale)
    head, tail = banded(NX, NX, c)
    along_x = jnp.concatenate(
        [jnp.concatenate([head, tail], axis=1), jnp.concatenate([head, jnp.zeros_like(tail)], axis=1)], axis=0
    )
    head, tail = banded(NX, NY, c)
    along_y = jnp.concatenate([head, head, tail], axis=1)

    def block(i, carry):
        at = pl.ds(pl.multiple_of(i * NX, NX), NX)
        head, tail = two_parts(field_ref[at, :])
        both = dot_nn(jnp.concatenate([head, tail], axis=1), along_x)
        across = dot_nn(along_y, jnp.concatenate([head, tail, head], axis=0))
        planar_ref[at, :] = both[:, :NX] + both[:, NX:] + across
        return carry

    lax.fori_loop(0, orbitals * ROWS // NX, block, 0, unroll=4)

    def orbital(o, carry):
        base = o * ROWS
        spots = [pl.ds(pl.multiple_of(base + NY * j, NY), NY) for j in range(PLANES)]
        cells = [field_ref[s, :] for s in spots]
        for j in range(PLANES):
            total = planar_ref[spots[j], :] + cells[j] * v_scr[NY * j : NY * j + NY, :]
            if back is not None:
                total = total + back * start_ref[spots[j], :]
            for k in range(1, PLANES):
                others = [cells[i] for i in (j - k, j + k) if 0 <= i < PLANES]
                if others:
                    total = total + c[k] * sum(others[1:], others[0])
            out_ref[spots[j], :] = total
        return carry

    lax.fori_loop(0, orbitals, orbital, 0, unroll=2)


def shift(x, by):
    return pltpu.roll(x, NX - by, 1)


def atom_sums(own, far, beyond):
    lane = lanes(own.shape)
    first, second = lane < OWNED, lane < 2 * OWNED
    sums = own + jnp.where(
        first,
        shift(own, 4 * OWNED) + shift(beyond, 2 * OWNED),
        jnp.where(second, shift(far, OWNED), pltpu.roll(far, OWNED, 1)),
    )
    energy = jnp.where(
        first, shift(own, 5 * OWNED), jnp.where(second, shift(own, 2 * OWNED), shift(far, OWNED))
    )
    return jnp.where(lane < KAM, sums * energy, 0.0)


def add_rest(out_ref, slab_ref, mate_ref, far_ref, proj_ref, coeff, nonlocal_ref, odd, scale, orbitals):
    head, tail = two_parts((coeff * scale)[:, :KAM])
    lhs = jnp.concatenate([head, head, tail], axis=1)

    def spread(pair, carry):
        row = 2 * pair
        rhs = jnp.concatenate([proj_ref[row + i] for i in (0, 1)], axis=1)
        both = dot_nn(lhs, rhs)
        for i in (0, 1):
            nonlocal_ref[pl.ds(row + i, orbitals, stride=ROWS), :] = both[:, i * NX : (i + 1) * NX]
        return carry

    lax.fori_loop(0, ROWS // 2, spread, 0, unroll=4)
    c = weights(scale)
    place = places(odd)

    def orbital(o, carry):
        base = o * ROWS
        spots = [pl.ds(pl.multiple_of(base + p, NY), NY) for p in place]
        mate = [mate_ref[s, :] for s in spots]
        beyond = [far_ref[s, :] for s in spots]
        for j in range(PLANES):
            total = slab_ref[spots[j], :] + nonlocal_ref[spots[j], :]
            for k in range(1, 7):
                terms = []
                if j - k < 0:
                    terms.append(mate[PLANES + j - k])
                if j + k >= PLANES:
                    terms.append(beyond[j + k - PLANES])
                if terms:
                    total = total + c[k] * sum(terms[1:], terms[0])
            out_ref[spots[j], :] = total
        return carry

    lax.fori_loop(0, orbitals, orbital, 0, unroll=2)


def first_kernel(
    place_ref, slab_ref, mate_ref, far_ref, proj_ref, own_msg, far_msg, beyond_msg, kb_ref,
    out_ref, own_out, mate_out, sums_ref, nonlocal_ref, *, orbitals, scale,
):
    sums = atom_sums(own_msg[...], far_msg[:orbitals, :], beyond_msg[:orbitals, :])
    sums_ref[...] = sums
    add_rest(out_ref, slab_ref, mate_ref, far_ref, proj_ref, sums, nonlocal_ref, place_ref[0], scale, orbitals)
    put_messages(project(out_ref, proj_ref, orbitals), kb_ref, own_out, mate_out)
    lane = lanes(sums.shape)
    own_out[...] = jnp.where(lane < 6 * OWNED, own_out[...], jnp.where(lane < 7 * OWNED, pltpu.roll(sums, 6 * OWNED, 1), 0.0))


def far_first_kernel(
    place_ref, slab_ref, mate_ref, psi_ref, proj_ref, sums_ref, far_msg, out_ref, nonlocal_ref, *, orbitals, scale
):
    sums, far = sums_ref[...], far_msg[...]
    lane = lanes(sums.shape)
    far_sums = jnp.where(
        lane < OWNED, shift(far, 6 * OWNED), jnp.where(lane < 2 * OWNED, shift(sums, OWNED), pltpu.roll(sums, OWNED, 1))
    )
    add_rest(out_ref, slab_ref, mate_ref, psi_ref, proj_ref, far_sums, nonlocal_ref, 1 - place_ref[0], scale, orbitals)


def second_kernel(
    place_ref, slab_ref, mate_ref, far_ref, proj_ref, own_msg, far_msg, beyond_msg, out_ref, *rest, orbitals, scale
):
    *chunk_refs, nonlocal_ref = rest
    coeff = atom_sums(own_msg[...], far_msg[...], beyond_msg[...])
    add_rest(out_ref, slab_ref, mate_ref, far_ref, proj_ref, coeff, nonlocal_ref, place_ref[0], scale, orbitals)
    share = ROWS // len(chunk_refs)
    for m, chunk_ref in enumerate(chunk_refs):
        at = (place_ref[1] ^ m) * share
        for i in range(share):
            chunk_ref[i] = row_of(out_ref, at + i, orbitals)


def gram_kernel(place_ref, *refs, orbitals, width, scale):
    *block_refs, out_ref, head_ref, tail_ref, gram_ref = refs
    for m, block_ref in enumerate(block_refs):
        at = pl.ds(pl.multiple_of((place_ref[1] ^ m) * orbitals, orbitals), orbitals)
        for i in range(block_ref.shape[0]):
            head, tail = two_parts(block_ref[i])
            head_ref[at, i * NX : (i + 1) * NX] = head
            tail_ref[at, i * NX : (i + 1) * NX] = tail
    head = head_ref[...]
    cross = dot_nt(tail_ref[...], head)
    gram_ref[...] = (dot_nt(head, head) + cross + cross.T) * scale
    n = gram_ref.shape[0]
    groups = len(block_refs)
    parts = [gram_ref[pl.ds(t, n // width, stride=width), :] for t in range(width)]
    lane = lanes(parts[0].shape)
    for q in range(groups):
        row = parts[0] if q == 0 else pltpu.roll(parts[0], n - orbitals * q, 1)
        for t in range(1, width):
            by = (orbitals * (t - q)) % n
            row = jnp.where(lane < orbitals * t, row, pltpu.roll(parts[t], by, 1) if by else parts[t])
        out_ref[pl.ds(q, n // width, stride=groups), :] = row


def params(mib):
    return pltpu.CompilerParams(vmem_limit_bytes=mib * 2**20)


def on_device(psi_in, v_local, proj_index, proj_value, kb_energy):
    orbitals = psi_in.shape[0]
    slabs = lax.axis_size("grid")
    groups = lax.axis_size("orb")
    mates = [(i, i ^ 1) for i in range(slabs)]
    fars = [(i, (i + 1 if i % 2 else i - 1) % slabs) for i in range(slabs)]
    n = orbitals * groups
    width = n // slabs

    def swap(x, pairs):
        return lax.ppermute(x, "grid", pairs)

    place = jnp.stack([lax.axis_index("grid") % 2, lax.axis_index("orb")]).astype(jnp.int32)
    field_shape = jax.ShapeDtypeStruct((orbitals * ROWS, NX), F32)
    message_shape = jax.ShapeDtypeStruct((orbitals, NX), F32)
    psi = psi_in.reshape(orbitals * ROWS, NX)
    v = v_local.reshape(ROWS, NX)
    kb = kb_energy.reshape(1, OWNED)
    kb = jnp.pad(kb, ((0, 0), (KAM, 0))) + jnp.zeros((1, KAM + OWNED), F32)
    kb = jnp.pad(jnp.concatenate([kb, kb[:, 2 * OWNED :]], axis=1), ((0, 0), (0, NX - 6 * OWNED)))

    def kernel(body, name, outs, scratch, mib, *operands, scalars=True, **statics):
        return pl.pallas_call(
            functools.partial(body, **statics),
            out_shape=outs,
            in_specs=[SMEM] * scalars + [VMEM] * len(operands),
            out_specs=jax.tree.map(lambda _: VMEM, outs),
            scratch_shapes=scratch,
            compiler_params=params(mib),
            cost_estimate=pl.CostEstimate(flops=10**9, bytes_accessed=10**7, transcendentals=0),
            name=name,
        )(*([place] * scalars), *operands)

    field_scratch = pltpu.VMEM((orbitals * ROWS, NX), F32)
    proj_shape = jax.ShapeDtypeStruct((ROWS, 3 * KAM, NX), BF16)
    proj_scratch = [pltpu.VMEM((2, ROWS * OWNED, SLOTS * PTS), BF16)]

    def slab(field, potential, scale, back, *start):
        scratch = [pltpu.VMEM((ROWS, NX), F32), field_scratch]
        return kernel(
            slab_kernel, "slab", field_shape, scratch, 8, field, potential, *start,
            scalars=False, orbitals=orbitals, scale=scale, back=back,
        )

    first_scale, scale = SIGMA / HALF_WIDTH, 2.0 * SIGMA_TWO / HALF_WIDTH
    far = swap(psi, fars)
    mate = swap(psi, mates)
    proj, own, to_mate = kernel(
        projector_kernel, "projectors", (proj_shape, message_shape, message_shape), proj_scratch, 16,
        proj_index, proj_value, kb, psi, orbitals=orbitals,
    )
    own = own + swap(to_mate, mates)
    values = proj_value.reshape(3 * OWNED, PTS)
    indices = proj_index.astype(F32).reshape(3 * SLOTS, PTS)
    value_at = orbitals + ROWS
    index_at = value_at + 3 * OWNED
    message = jnp.concatenate([own, v, values, indices], axis=0)
    from_far = swap(message, fars)
    message, field = lax.optimization_barrier((message, psi))
    local = slab(field, v, first_scale, None)
    local, mate = lax.optimization_barrier((local, mate))
    far_mate = swap(mate, fars)
    from_far, local = lax.optimization_barrier((from_far, local))
    from_beyond = swap(from_far, mates)
    first, own, to_mate, sums = kernel(
        first_kernel, "first", (field_shape, message_shape, message_shape, message_shape), [field_scratch], 16,
        local, mate, far, proj, message[:orbitals], from_far, from_beyond, kb, orbitals=orbitals, scale=first_scale,
    )
    first_mate = swap(first, mates)
    own = own + swap(to_mate, mates)
    far_again = swap(own, fars)
    own, from_far, far, first = lax.optimization_barrier((own, from_far, far, first))
    far_proj = kernel(
        far_projector_kernel, "far_projectors", proj_shape, proj_scratch, 16, from_far,
        index_at=index_at, value_at=value_at,
    )
    far_local = slab(far, from_far[orbitals:value_at], first_scale, None)
    far_again, far_proj, far_local = lax.optimization_barrier((far_again, far_proj, far_local))
    beyond_again = swap(far_again, mates)
    first, far_mate = lax.optimization_barrier((first, far_mate))
    local = slab(first, v, scale, -SIGMA * SIGMA_TWO, psi)
    first_far = kernel(
        far_first_kernel, "far_first", field_shape, [field_scratch], 16,
        far_local, far_mate, psi, far_proj, sums, far_again, orbitals=orbitals, scale=first_scale,
    )
    chunk = jax.ShapeDtypeStruct((ROWS // groups, orbitals, NX), F32)
    filtered, *blocks = kernel(
        second_kernel, "second", (field_shape,) + (chunk,) * groups, [field_scratch], 16,
        local, first_mate, first_far, proj, own, far_again, beyond_again, orbitals=orbitals, scale=scale,
    )
    for m in reversed(range(1, groups)):
        blocks[m] = lax.ppermute(blocks[m], "orb", [(i, i ^ m) for i in range(groups)])
    tiles = pl.pallas_call(
        functools.partial(gram_kernel, orbitals=orbitals, width=width, scale=1.0 / (slabs * ROWS * NX)),
        out_shape=jax.ShapeDtypeStruct((slabs * groups, n), F32),
        in_specs=[SMEM] + [VMEM] * groups,
        out_specs=VMEM,
        scratch_shapes=[pltpu.VMEM((n, ROWS // groups * NX), BF16)] * 2 + [pltpu.VMEM((n, n), F32)],
        compiler_params=params(8),
        cost_estimate=pl.CostEstimate(flops=10**8, bytes_accessed=10**6, transcendentals=0),
        name="gram",
    )(place, *blocks)
    tiles = lax.all_to_all(tiles, ("grid", "orb"), 0, 0, tiled=True)
    gram = jnp.sum(tiles, axis=0)[: width * orbitals].reshape(width, orbitals).T
    return filtered.reshape(psi_in.shape), gram


def solution(mesh):
    placed = (
        P("orb", "grid", None, None),
        P("grid", None, None),
        P("grid", None, None),
        P("grid", None, None, None),
        P("grid", None),
    )
    return jax.shard_map(
        on_device,
        mesh=mesh,
        in_specs=placed,
        out_specs=(P("orb", "grid", None, None), P("orb", "grid")),
        check_vma=False,
    )
```

```python
import functools

import jax
import jax.numpy as jnp
from jax import lax
from jax.experimental import pallas as pl
from jax.experimental.pallas import tpu as pltpu
from jax.sharding import PartitionSpec as P

LAP_COEF = (
    -5369.0 / 1800.0,
    12.0 / 7.0,
    -15.0 / 56.0,
    10.0 / 189.0,
    -1.0 / 112.0,
    2.0 / 1925.0,
    -1.0 / 16632.0,
)
HALF_WIDTH = 6.0
CENTRE = 8.0
SIGMA = HALF_WIDTH / (-3.0 - CENTRE)
SIGMA_TWO = 1.0 / (2.0 / SIGMA - SIGMA)

NX = 128
NY = 8
PLANES = 6
ROWS = PLANES * NY
SLOTS = 4
PROJ = 4
OWNED = SLOTS * PROJ
KAM = 3 * OWNED
PTS = 128

F32 = jnp.float32
BF16 = jnp.bfloat16
VMEM = pl.BlockSpec(memory_space=pltpu.VMEM)
SMEM = pl.BlockSpec(memory_space=pltpu.SMEM)
ANY = pl.BlockSpec(memory_space=pl.ANY)


def two_parts(x):
    head = x.astype(BF16)
    return head, (x - head.astype(F32)).astype(BF16)


def dot_nt(lhs, rhs):
    return lax.dot_general(lhs, rhs, (((1,), (1,)), ((), ())), preferred_element_type=F32)


def dot_nn(lhs, rhs):
    return lax.dot_general(lhs, rhs, (((1,), (0,)), ((), ())), preferred_element_type=F32)


def row_of(field_ref, row, orbitals):
    return field_ref[pl.ds(row, orbitals, stride=ROWS), :]


def lanes(shape):
    return lax.broadcasted_iota(jnp.int32, shape, 1)


def project(field_ref, proj_ref, orbitals):
    def step(pair, acc):
        row = 2 * pair
        points = jnp.concatenate([row_of(field_ref, row + i, orbitals) for i in (0, 1)], axis=1)
        head, tail = two_parts(points)
        lhs = jnp.concatenate([head, tail], axis=0)
        rhs = jnp.concatenate([proj_ref[row + i, :NX, :] for i in (0, 1)], axis=1)
        return acc + dot_nt(lhs, rhs)

    acc = lax.fori_loop(0, ROWS // 2, step, jnp.zeros((2 * orbitals, NX), F32), unroll=4)
    acc = acc[:orbitals] + acc[orbitals:]
    return jnp.where(lanes(acc.shape) < KAM, acc + pltpu.roll(acc, NX - KAM, 1), 0.0)


def put_messages(part, kb_ref, own_ref, mate_ref):
    lane = lanes(part.shape)
    kb = jnp.broadcast_to(kb_ref[...], part.shape)
    own_ref[...] = jnp.where(lane < KAM, part, jnp.where(lane < KAM + OWNED, kb, 0.0))
    mate = jnp.where(lane < 4 * OWNED, pltpu.roll(part, 3 * OWNED, 1), kb)
    mate = jnp.where(lane < 2 * OWNED, pltpu.roll(part, OWNED, 1), mate)
    mate = jnp.where(lane < 5 * OWNED, jnp.where(lane < 4 * OWNED, mate, pltpu.roll(part, 3 * OWNED, 1)), kb)
    sent = ((lane >= OWNED) & (lane < 2 * OWNED)) | ((lane >= 4 * OWNED) & (lane < 6 * OWNED))
    mate_ref[...] = jnp.where(sent, mate, 0.0)


def fill_projectors(even, index_of, value_of, proj_ref, lhs_ref):
    slot = lax.broadcasted_iota(jnp.int32, (OWNED, PTS), 0) // PROJ
    lane_no = lax.broadcasted_iota(jnp.int32, (NX, PTS), 0)
    row_no = lax.broadcasted_iota(jnp.int32, (ROWS, OWNED, PTS), 0)
    for frame in range(3):
        piece = frame + even * (2 - 2 * frame)
        index = index_of(piece)
        value = value_of(piece)
        parts = [p.astype(F32) for p in two_parts(value)]
        hits = []
        for a in range(SLOTS):
            mine = index[a : a + 1, :]
            row = jnp.where(slot == a, jnp.broadcast_to(mine >> 7, (OWNED, PTS)), -1)
            here = row_no == row[None]
            for i, part in enumerate(parts):
                chosen = jnp.where(here, part[None], 0.0)
                lhs_ref[i, :, a * PTS : (a + 1) * PTS] = chosen.reshape(ROWS * OWNED, PTS).astype(BF16)
            hits.append(jnp.where(lane_no == jnp.broadcast_to(mine & (NX - 1), (NX, PTS)), 1.0, 0.0).astype(BF16))
        rhs = jnp.concatenate(hits, axis=1)
        dense = dot_nt(lhs_ref[0], rhs) + dot_nt(lhs_ref[1], rhs)
        head, tail = two_parts(dense.reshape(ROWS, OWNED, NX))
        at = frame * OWNED
        proj_ref[:, at : at + OWNED, :] = head
        proj_ref[:, KAM + at : KAM + at + OWNED, :] = tail
        proj_ref[:, 2 * KAM + at : 2 * KAM + at + OWNED, :] = head


def projector_kernel(place_ref, index_ref, value_ref, kb_ref, psi_ref, proj_ref, own_ref, mate_ref, lhs_ref, *, orbitals):
    def value_of(piece):
        return jnp.concatenate([value_ref[piece, a] for a in range(SLOTS)], axis=0)

    fill_projectors(1 - place_ref[0], lambda piece: index_ref[piece], value_of, proj_ref, lhs_ref)
    put_messages(project(psi_ref, proj_ref, orbitals), kb_ref, own_ref, mate_ref)


def far_projector_kernel(place_ref, message_ref, proj_ref, lhs_ref, *, index_at, value_at):
    def index_of(piece):
        return message_ref[pl.ds(index_at + piece * SLOTS, SLOTS), :].astype(jnp.int32)

    def value_of(piece):
        return message_ref[pl.ds(pl.multiple_of(value_at + piece * OWNED, 8), OWNED), :]

    fill_projectors(place_ref[0], index_of, value_of, proj_ref, lhs_ref)


def weights(scale):
    return [-0.5 * scale * x for x in LAP_COEF]


def places(odd):
    return [NY * ((PLANES - 1 - j) + odd * (2 * j - PLANES + 1)) for j in range(PLANES)]


def banded(size, period, c):
    i, j = (lax.broadcasted_iota(jnp.int32, (size, size), d) for d in (0, 1))
    ahead = (j - i) & (period - 1)
    matrix = jnp.zeros((size, size), F32)
    for k in range(1, 7):
        for by in (k, -k):
            matrix = matrix + jnp.where(ahead == by % period, c[k], 0.0)
    return two_parts(jnp.where(i // period == j // period, matrix, 0.0))


def slab_kernel(field_ref, v_ref, *rest, orbitals, scale, back):
    start_ref = rest[0] if back is not None else None
    out_ref, v_scr, planar_ref = rest[-3:]
    v_scr[...] = (v_ref[...] - (CENTRE + 1.5 * LAP_COEF[0])) * scale
    c = weights(scale)
    head, tail = banded(NX, NX, c)
    along_x = jnp.concatenate(
        [jnp.concatenate([head, tail], axis=1), jnp.concatenate([head, jnp.zeros_like(tail)], axis=1)], axis=0
    )
    head, tail = banded(NX, NY, c)
    along_y = jnp.concatenate([head, head, tail], axis=1)

    def block(i, carry):
        at = pl.ds(pl.multiple_of(i * NX, NX), NX)
        head, tail = two_parts(field_ref[at, :])
        both = dot_nn(jnp.concatenate([head, tail], axis=1), along_x)
        across = dot_nn(along_y, jnp.concatenate([head, tail, head], axis=0))
        planar_ref[at, :] = both[:, :NX] + both[:, NX:] + across
        return carry

    lax.fori_loop(0, orbitals * ROWS // NX, block, 0, unroll=4)

    def orbital(o, carry):
        base = o * ROWS
        spots = [pl.ds(pl.multiple_of(base + NY * j, NY), NY) for j in range(PLANES)]
        cells = [field_ref[s, :] for s in spots]
        for j in range(PLANES):
            total = planar_ref[spots[j], :] + cells[j] * v_scr[NY * j : NY * j + NY, :]
            if back is not None:
                total = total + back * start_ref[spots[j], :]
            for k in range(1, PLANES):
                others = [cells[i] for i in (j - k, j + k) if 0 <= i < PLANES]
                if others:
                    total = total + c[k] * sum(others[1:], others[0])
            out_ref[spots[j], :] = total
        return carry

    lax.fori_loop(0, orbitals, orbital, 0, unroll=2)


def shift(x, by):
    return pltpu.roll(x, NX - by, 1)


def atom_sums(own, far, beyond):
    lane = lanes(own.shape)
    first, second = lane < OWNED, lane < 2 * OWNED
    sums = own + jnp.where(
        first,
        shift(own, 4 * OWNED) + shift(beyond, 2 * OWNED),
        jnp.where(second, shift(far, OWNED), pltpu.roll(far, OWNED, 1)),
    )
    energy = jnp.where(
        first, shift(own, 5 * OWNED), jnp.where(second, shift(own, 2 * OWNED), shift(far, OWNED))
    )
    return jnp.where(lane < KAM, sums * energy, 0.0)


def add_rest(
    out_ref, slab_ref, mate_ref, far_ref, proj_ref, coeff, nonlocal_ref, odd, scale, orbitals, until_here=None
):
    head, tail = two_parts((coeff * scale)[:, :KAM])
    lhs = jnp.concatenate([head, head, tail], axis=1)

    def spread(pair, carry):
        row = 2 * pair
        rhs = jnp.concatenate([proj_ref[row + i] for i in (0, 1)], axis=1)
        both = dot_nn(lhs, rhs)
        for i in (0, 1):
            nonlocal_ref[pl.ds(row + i, orbitals, stride=ROWS), :] = both[:, i * NX : (i + 1) * NX]
        return carry

    lax.fori_loop(0, ROWS // 2, spread, 0, unroll=4)
    if until_here is not None:
        until_here()
    c = weights(scale)
    place = places(odd)

    def orbital(o, carry):
        base = o * ROWS
        spots = [pl.ds(pl.multiple_of(base + p, NY), NY) for p in place]
        mate = [mate_ref[s, :] for s in spots]
        beyond = [far_ref[s, :] for s in spots]
        for j in range(PLANES):
            total = slab_ref[spots[j], :] + nonlocal_ref[spots[j], :]
            for k in range(1, 7):
                terms = []
                if j - k < 0:
                    terms.append(mate[PLANES + j - k])
                if j + k >= PLANES:
                    terms.append(beyond[j + k - PLANES])
                if terms:
                    total = total + c[k] * sum(terms[1:], terms[0])
            out_ref[spots[j], :] = total
        return carry

    lax.fori_loop(0, orbitals, orbital, 0, unroll=2)


def first_kernel(
    place_ref, slab_ref, mate_ref, far_arrived, proj_ref, own_msg, far_msg, beyond_msg, kb_ref,
    out_ref, own_out, mate_out, sums_ref, far_ref, nonlocal_ref, arrival, *, orbitals, scale,
):
    fetch = pltpu.make_async_copy(far_arrived, far_ref, arrival)
    fetch.start()
    sums = atom_sums(own_msg[...], far_msg[:orbitals, :], beyond_msg[:orbitals, :])
    sums_ref[...] = sums
    add_rest(
        out_ref, slab_ref, mate_ref, far_ref, proj_ref, sums, nonlocal_ref, place_ref[0], scale, orbitals, fetch.wait
    )
    put_messages(project(out_ref, proj_ref, orbitals), kb_ref, own_out, mate_out)
    lane = lanes(sums.shape)
    own_out[...] = jnp.where(lane < 6 * OWNED, own_out[...], jnp.where(lane < 7 * OWNED, pltpu.roll(sums, 6 * OWNED, 1), 0.0))


def far_first_kernel(
    place_ref, slab_ref, mate_ref, psi_ref, proj_ref, sums_ref, far_msg, out_ref, nonlocal_ref, *, orbitals, scale
):
    sums, far = sums_ref[...], far_msg[...]
    lane = lanes(sums.shape)
    far_sums = jnp.where(
        lane < OWNED, shift(far, 6 * OWNED), jnp.where(lane < 2 * OWNED, shift(sums, OWNED), pltpu.roll(sums, OWNED, 1))
    )
    add_rest(out_ref, slab_ref, mate_ref, psi_ref, proj_ref, far_sums, nonlocal_ref, 1 - place_ref[0], scale, orbitals)


def second_kernel(
    place_ref, slab_ref, mate_ref, far_ref, proj_ref, own_msg, far_msg, beyond_msg, out_ref, *rest, orbitals, scale
):
    *chunk_refs, nonlocal_ref = rest
    coeff = atom_sums(own_msg[...], far_msg[...], beyond_msg[...])
    add_rest(out_ref, slab_ref, mate_ref, far_ref, proj_ref, coeff, nonlocal_ref, place_ref[0], scale, orbitals)
    share = ROWS // len(chunk_refs)
    for m, chunk_ref in enumerate(chunk_refs):
        at = (place_ref[1] ^ m) * share
        for i in range(share):
            chunk_ref[i] = row_of(out_ref, at + i, orbitals)


def gram_kernel(place_ref, *refs, orbitals, width, scale):
    *block_refs, out_ref, head_ref, tail_ref, gram_ref = refs
    for m, block_ref in enumerate(block_refs):
        at = pl.ds(pl.multiple_of((place_ref[1] ^ m) * orbitals, orbitals), orbitals)
        for i in range(block_ref.shape[0]):
            head, tail = two_parts(block_ref[i])
            head_ref[at, i * NX : (i + 1) * NX] = head
            tail_ref[at, i * NX : (i + 1) * NX] = tail
    head = head_ref[...]
    cross = dot_nt(tail_ref[...], head)
    gram_ref[...] = (dot_nt(head, head) + cross + cross.T) * scale
    n = gram_ref.shape[0]
    groups = len(block_refs)
    parts = [gram_ref[pl.ds(t, n // width, stride=width), :] for t in range(width)]
    lane = lanes(parts[0].shape)
    for q in range(groups):
        row = parts[0] if q == 0 else pltpu.roll(parts[0], n - orbitals * q, 1)
        for t in range(1, width):
            by = (orbitals * (t - q)) % n
            row = jnp.where(lane < orbitals * t, row, pltpu.roll(parts[t], by, 1) if by else parts[t])
        out_ref[pl.ds(q, n // width, stride=groups), :] = row


def params(mib):
    return pltpu.CompilerParams(vmem_limit_bytes=mib * 2**20)


def on_device(psi_in, v_local, proj_index, proj_value, kb_energy):
    orbitals = psi_in.shape[0]
    slabs = lax.axis_size("grid")
    groups = lax.axis_size("orb")
    mates = [(i, i ^ 1) for i in range(slabs)]
    fars = [(i, (i + 1 if i % 2 else i - 1) % slabs) for i in range(slabs)]
    n = orbitals * groups
    width = n // slabs

    def swap(x, pairs):
        return lax.ppermute(x, "grid", pairs)

    place = jnp.stack([lax.axis_index("grid") % 2, lax.axis_index("orb")]).astype(jnp.int32)
    field_shape = jax.ShapeDtypeStruct((orbitals * ROWS, NX), F32)
    message_shape = jax.ShapeDtypeStruct((orbitals, NX), F32)
    psi = psi_in.reshape(orbitals * ROWS, NX)
    v = v_local.reshape(ROWS, NX)
    kb = kb_energy.reshape(1, OWNED)
    kb = jnp.pad(kb, ((0, 0), (KAM, 0))) + jnp.zeros((1, KAM + OWNED), F32)
    kb = jnp.pad(jnp.concatenate([kb, kb[:, 2 * OWNED :]], axis=1), ((0, 0), (0, NX - 6 * OWNED)))

    def kernel(body, name, outs, scratch, mib, *operands, scalars=True, left=(), flops=10**9, **statics):
        return pl.pallas_call(
            functools.partial(body, **statics),
            out_shape=outs,
            in_specs=[SMEM] * scalars + [ANY if i in left else VMEM for i in range(len(operands))],
            out_specs=jax.tree.map(lambda _: VMEM, outs),
            scratch_shapes=scratch,
            compiler_params=params(mib),
            cost_estimate=pl.CostEstimate(flops=flops, bytes_accessed=10**7, transcendentals=0),
            name=name,
        )(*([place] * scalars), *operands)

    field_scratch = pltpu.VMEM((orbitals * ROWS, NX), F32)
    proj_shape = jax.ShapeDtypeStruct((ROWS, 3 * KAM, NX), BF16)
    proj_scratch = [pltpu.VMEM((2, ROWS * OWNED, SLOTS * PTS), BF16)]

    def slab(field, potential, scale, back, *start):
        scratch = [pltpu.VMEM((ROWS, NX), F32), field_scratch]
        return kernel(
            slab_kernel, "slab", field_shape, scratch, 8, field, potential, *start,
            scalars=False, orbitals=orbitals, scale=scale, back=back,
        )

    first_scale, scale = SIGMA / HALF_WIDTH, 2.0 * SIGMA_TWO / HALF_WIDTH
    far = swap(psi, fars)
    mate = swap(psi, mates)
    proj, own, to_mate = kernel(
        projector_kernel, "projectors", (proj_shape, message_shape, message_shape), proj_scratch, 16,
        proj_index, proj_value, kb, psi, orbitals=orbitals,
    )
    own = own + swap(to_mate, mates)
    values = proj_value.reshape(3 * OWNED, PTS)
    indices = proj_index.astype(F32).reshape(3 * SLOTS, PTS)
    value_at = orbitals + ROWS
    index_at = value_at + 3 * OWNED
    message = jnp.concatenate([own, v, values, indices], axis=0)
    from_far = swap(message, fars)
    message, field = lax.optimization_barrier((message, psi))
    local = slab(field, v, first_scale, None)
    local, mate = lax.optimization_barrier((local, mate))
    far_mate = swap(mate, fars)
    from_far, local = lax.optimization_barrier((from_far, local))
    from_beyond = swap(from_far, mates)
    first, own, to_mate, sums, far = kernel(
        first_kernel, "first", (field_shape, message_shape, message_shape, message_shape, field_shape),
        [field_scratch, pltpu.SemaphoreType.DMA(())], 16,
        local, mate, far, proj, message[:orbitals], from_far, from_beyond, kb,
        left=(2,), orbitals=orbitals, scale=first_scale,
    )
    first_mate = swap(first, mates)
    own = own + swap(to_mate, mates)
    far_again = swap(own, fars)
    own, from_far, far, first = lax.optimization_barrier((own, from_far, far, first))
    far_proj = kernel(
        far_projector_kernel, "far_projectors", proj_shape, proj_scratch, 16, from_far,
        index_at=index_at, value_at=value_at,
    )
    far_local = slab(far, from_far[orbitals:value_at], first_scale, None)
    local = slab(first, v, scale, -SIGMA * SIGMA_TWO, psi)
    far_again, far_proj, far_local, local = lax.optimization_barrier((far_again, far_proj, far_local, local))
    beyond_again = swap(far_again, mates)
    first_far = kernel(
        far_first_kernel, "far_first", field_shape, [field_scratch], 16,
        far_local, far_mate, psi, far_proj, sums, far_again, flops=20 * 10**8,
        orbitals=orbitals, scale=first_scale,
    )
    chunk = jax.ShapeDtypeStruct((ROWS // groups, orbitals, NX), F32)
    filtered, *blocks = kernel(
        second_kernel, "second", (field_shape,) + (chunk,) * groups, [field_scratch], 16,
        local, first_mate, first_far, proj, own, far_again, beyond_again, orbitals=orbitals, scale=scale,
    )
    for m in reversed(range(1, groups)):
        blocks[m] = lax.ppermute(blocks[m], "orb", [(i, i ^ m) for i in range(groups)])
    tiles = pl.pallas_call(
        functools.partial(gram_kernel, orbitals=orbitals, width=width, scale=1.0 / (slabs * ROWS * NX)),
        out_shape=jax.ShapeDtypeStruct((slabs * groups, n), F32),
        in_specs=[SMEM] + [VMEM] * groups,
        out_specs=VMEM,
        scratch_shapes=[pltpu.VMEM((n, ROWS // groups * NX), BF16)] * 2 + [pltpu.VMEM((n, n), F32)],
        compiler_params=params(8),
        cost_estimate=pl.CostEstimate(flops=10**8, bytes_accessed=10**6, transcendentals=0),
        name="gram",
    )(place, *blocks)
    tiles = lax.all_to_all(tiles, ("grid", "orb"), 0, 0, tiled=True)
    gram = jnp.sum(tiles, axis=0)[: width * orbitals].reshape(width, orbitals).T
    return filtered.reshape(psi_in.shape), gram


def solution(mesh):
    placed = (
        P("orb", "grid", None, None),
        P("grid", None, None),
        P("grid", None, None),
        P("grid", None, None, None),
        P("grid", None),
    )
    return jax.shard_map(
        on_device,
        mesh=mesh,
        in_specs=placed,
        out_specs=(P("orb", "grid", None, None), P("orb", "grid")),
        check_vma=False,
    )
```

```python
import functools

import jax
import jax.numpy as jnp
from jax import lax
from jax.experimental import pallas as pl
from jax.experimental.pallas import tpu as pltpu
from jax.sharding import PartitionSpec as P

LAP_COEF = (
    -5369.0 / 1800.0,
    12.0 / 7.0,
    -15.0 / 56.0,
    10.0 / 189.0,
    -1.0 / 112.0,
    2.0 / 1925.0,
    -1.0 / 16632.0,
)
HALF_WIDTH = 6.0
CENTRE = 8.0
SIGMA = HALF_WIDTH / (-3.0 - CENTRE)
SIGMA_TWO = 1.0 / (2.0 / SIGMA - SIGMA)

NX = 128
NY = 8
PLANES = 6
ROWS = PLANES * NY
SLOTS = 4
PROJ = 4
OWNED = SLOTS * PROJ
KAM = 3 * OWNED
PTS = 128

F32 = jnp.float32
BF16 = jnp.bfloat16
VMEM = pl.BlockSpec(memory_space=pltpu.VMEM)
SMEM = pl.BlockSpec(memory_space=pltpu.SMEM)
ANY = pl.BlockSpec(memory_space=pl.ANY)


def two_parts(x):
    head = x.astype(BF16)
    return head, (x - head.astype(F32)).astype(BF16)


def dot_nt(lhs, rhs):
    return lax.dot_general(lhs, rhs, (((1,), (1,)), ((), ())), preferred_element_type=F32)


def dot_nn(lhs, rhs):
    return lax.dot_general(lhs, rhs, (((1,), (0,)), ((), ())), preferred_element_type=F32)


def row_of(field_ref, row, orbitals):
    return field_ref[pl.ds(row, orbitals, stride=ROWS), :]


def lanes(shape):
    return lax.broadcasted_iota(jnp.int32, shape, 1)


def project(field_ref, proj_ref, orbitals):
    def step(pair, acc):
        row = 2 * pair
        points = jnp.concatenate([row_of(field_ref, row + i, orbitals) for i in (0, 1)], axis=1)
        head, tail = two_parts(points)
        lhs = jnp.concatenate([head, tail], axis=0)
        rhs = jnp.concatenate([proj_ref[row + i, :NX, :] for i in (0, 1)], axis=1)
        return acc + dot_nt(lhs, rhs)

    acc = lax.fori_loop(0, ROWS // 2, step, jnp.zeros((2 * orbitals, NX), F32), unroll=12)
    acc = acc[:orbitals] + acc[orbitals:]
    return jnp.where(lanes(acc.shape) < KAM, acc + pltpu.roll(acc, NX - KAM, 1), 0.0)


def put_messages(part, kb_ref, own_ref, mate_ref):
    lane = lanes(part.shape)
    kb = jnp.broadcast_to(kb_ref[...], part.shape)
    own_ref[...] = jnp.where(lane < KAM, part, jnp.where(lane < KAM + OWNED, kb, 0.0))
    mate = jnp.where(lane < 4 * OWNED, pltpu.roll(part, 3 * OWNED, 1), kb)
    mate = jnp.where(lane < 2 * OWNED, pltpu.roll(part, OWNED, 1), mate)
    mate = jnp.where(lane < 5 * OWNED, jnp.where(lane < 4 * OWNED, mate, pltpu.roll(part, 3 * OWNED, 1)), kb)
    sent = ((lane >= OWNED) & (lane < 2 * OWNED)) | ((lane >= 4 * OWNED) & (lane < 6 * OWNED))
    mate_ref[...] = jnp.where(sent, mate, 0.0)


def fill_projectors(even, index_of, value_of, proj_ref, lhs_ref):
    slot = lax.broadcasted_iota(jnp.int32, (OWNED, PTS), 0) // PROJ
    lane_no = lax.broadcasted_iota(jnp.int32, (NX, PTS), 0)
    row_no = lax.broadcasted_iota(jnp.int32, (ROWS, OWNED, PTS), 0)
    for frame in range(3):
        piece = frame + even * (2 - 2 * frame)
        index = index_of(piece)
        value = value_of(piece)
        parts = [p.astype(F32) for p in two_parts(value)]
        hits = []
        for a in range(SLOTS):
            mine = index[a : a + 1, :]
            row = jnp.where(slot == a, jnp.broadcast_to(mine >> 7, (OWNED, PTS)), -1)
            here = row_no == row[None]
            for i, part in enumerate(parts):
                chosen = jnp.where(here, part[None], 0.0)
                lhs_ref[i, :, a * PTS : (a + 1) * PTS] = chosen.reshape(ROWS * OWNED, PTS).astype(BF16)
            hits.append(jnp.where(lane_no == jnp.broadcast_to(mine & (NX - 1), (NX, PTS)), 1.0, 0.0).astype(BF16))
        rhs = jnp.concatenate(hits, axis=1)
        dense = dot_nt(lhs_ref[0], rhs) + dot_nt(lhs_ref[1], rhs)
        head, tail = two_parts(dense.reshape(ROWS, OWNED, NX))
        at = frame * OWNED
        proj_ref[:, at : at + OWNED, :] = head
        proj_ref[:, KAM + at : KAM + at + OWNED, :] = tail
        proj_ref[:, 2 * KAM + at : 2 * KAM + at + OWNED, :] = head


def projector_kernel(place_ref, index_ref, value_ref, kb_ref, psi_ref, proj_ref, own_ref, mate_ref, lhs_ref, *, orbitals):
    def value_of(piece):
        return jnp.concatenate([value_ref[piece, a] for a in range(SLOTS)], axis=0)

    fill_projectors(1 - place_ref[0], lambda piece: index_ref[piece], value_of, proj_ref, lhs_ref)
    put_messages(project(psi_ref, proj_ref, orbitals), kb_ref, own_ref, mate_ref)


def far_projector_kernel(place_ref, message_ref, proj_ref, lhs_ref, *, index_at, value_at):
    def index_of(piece):
        return message_ref[pl.ds(index_at + piece * SLOTS, SLOTS), :].astype(jnp.int32)

    def value_of(piece):
        return message_ref[pl.ds(pl.multiple_of(value_at + piece * OWNED, 8), OWNED), :]

    fill_projectors(place_ref[0], index_of, value_of, proj_ref, lhs_ref)


def weights(scale):
    return [-0.5 * scale * x for x in LAP_COEF]


def places(odd):
    return [NY * ((PLANES - 1 - j) + odd * (2 * j - PLANES + 1)) for j in range(PLANES)]


def banded(size, period, c):
    i, j = (lax.broadcasted_iota(jnp.int32, (size, size), d) for d in (0, 1))
    ahead = (j - i) & (period - 1)
    matrix = jnp.zeros((size, size), F32)
    for k in range(1, 7):
        for by in (k, -k):
            matrix = matrix + jnp.where(ahead == by % period, c[k], 0.0)
    return two_parts(jnp.where(i // period == j // period, matrix, 0.0))


def slab_kernel(field_ref, v_ref, *rest, orbitals, scale, back):
    start_ref = rest[0] if back is not None else None
    out_ref, v_scr, planar_ref = rest[-3:]
    v_scr[...] = (v_ref[...] - (CENTRE + 1.5 * LAP_COEF[0])) * scale
    c = weights(scale)
    head, tail = banded(NX, NX, c)
    along_x = jnp.concatenate(
        [jnp.concatenate([head, tail], axis=1), jnp.concatenate([head, jnp.zeros_like(tail)], axis=1)], axis=0
    )
    head, tail = banded(NX, NY, c)
    along_y = jnp.concatenate([head, head, tail], axis=1)

    def block(i, carry):
        at = pl.ds(pl.multiple_of(i * NX, NX), NX)
        head, tail = two_parts(field_ref[at, :])
        both = dot_nn(jnp.concatenate([head, tail], axis=1), along_x)
        across = dot_nn(along_y, jnp.concatenate([head, tail, head], axis=0))
        planar_ref[at, :] = both[:, :NX] + both[:, NX:] + across
        return carry

    lax.fori_loop(0, orbitals * ROWS // NX, block, 0, unroll=4)

    def orbital(o, carry):
        base = o * ROWS
        spots = [pl.ds(pl.multiple_of(base + NY * j, NY), NY) for j in range(PLANES)]
        cells = [field_ref[s, :] for s in spots]
        for j in range(PLANES):
            total = planar_ref[spots[j], :] + cells[j] * v_scr[NY * j : NY * j + NY, :]
            if back is not None:
                total = total + back * start_ref[spots[j], :]
            for k in range(1, PLANES):
                others = [cells[i] for i in (j - k, j + k) if 0 <= i < PLANES]
                if others:
                    total = total + c[k] * sum(others[1:], others[0])
            out_ref[spots[j], :] = total
        return carry

    lax.fori_loop(0, orbitals, orbital, 0, unroll=4)


def shift(x, by):
    return pltpu.roll(x, NX - by, 1)


def atom_sums(own, far, beyond):
    lane = lanes(own.shape)
    first, second = lane < OWNED, lane < 2 * OWNED
    sums = own + jnp.where(
        first,
        shift(own, 4 * OWNED) + shift(beyond, 2 * OWNED),
        jnp.where(second, shift(far, OWNED), pltpu.roll(far, OWNED, 1)),
    )
    energy = jnp.where(
        first, shift(own, 5 * OWNED), jnp.where(second, shift(own, 2 * OWNED), shift(far, OWNED))
    )
    return jnp.where(lane < KAM, sums * energy, 0.0)


def add_rest(
    out_ref, slab_ref, mate_ref, far_ref, proj_ref, coeff, nonlocal_ref, odd, scale, orbitals, until_here=None
):
    head, tail = two_parts((coeff * scale)[:, :KAM])
    lhs = jnp.concatenate([head, head, tail], axis=1)

    def spread(pair, carry):
        row = 2 * pair
        rhs = jnp.concatenate([proj_ref[row + i] for i in (0, 1)], axis=1)
        both = dot_nn(lhs, rhs)
        for i in (0, 1):
            nonlocal_ref[pl.ds(row + i, orbitals, stride=ROWS), :] = both[:, i * NX : (i + 1) * NX]
        return carry

    lax.fori_loop(0, ROWS // 2, spread, 0, unroll=12)
    if until_here is not None:
        until_here()
    c = weights(scale)
    place = places(odd)

    def orbital(o, carry):
        base = o * ROWS
        spots = [pl.ds(pl.multiple_of(base + p, NY), NY) for p in place]
        mate = [mate_ref[s, :] for s in spots]
        beyond = [far_ref[s, :] for s in spots]
        for j in range(PLANES):
            total = slab_ref[spots[j], :] + nonlocal_ref[spots[j], :]
            for k in range(1, 7):
                terms = []
                if j - k < 0:
                    terms.append(mate[PLANES + j - k])
                if j + k >= PLANES:
                    terms.append(beyond[j + k - PLANES])
                if terms:
                    total = total + c[k] * sum(terms[1:], terms[0])
            out_ref[spots[j], :] = total
        return carry

    lax.fori_loop(0, orbitals, orbital, 0, unroll=4)


def first_kernel(
    place_ref, slab_ref, mate_ref, far_arrived, proj_ref, own_msg, far_msg, beyond_msg, kb_ref,
    out_ref, own_out, mate_out, sums_ref, far_ref, nonlocal_ref, arrival, *, orbitals, scale,
):
    fetch = pltpu.make_async_copy(far_arrived, far_ref, arrival)
    fetch.start()
    sums = atom_sums(own_msg[...], far_msg[:orbitals, :], beyond_msg[:orbitals, :])
    sums_ref[...] = sums
    add_rest(
        out_ref, slab_ref, mate_ref, far_ref, proj_ref, sums, nonlocal_ref, place_ref[0], scale, orbitals, fetch.wait
    )
    put_messages(project(out_ref, proj_ref, orbitals), kb_ref, own_out, mate_out)
    lane = lanes(sums.shape)
    own_out[...] = jnp.where(lane < 6 * OWNED, own_out[...], jnp.where(lane < 7 * OWNED, pltpu.roll(sums, 6 * OWNED, 1), 0.0))


def far_first_kernel(
    place_ref, slab_ref, mate_ref, psi_ref, proj_ref, sums_ref, far_msg, out_ref, nonlocal_ref, *, orbitals, scale
):
    sums, far = sums_ref[...], far_msg[...]
    lane = lanes(sums.shape)
    far_sums = jnp.where(
        lane < OWNED, shift(far, 6 * OWNED), jnp.where(lane < 2 * OWNED, shift(sums, OWNED), pltpu.roll(sums, OWNED, 1))
    )
    add_rest(out_ref, slab_ref, mate_ref, psi_ref, proj_ref, far_sums, nonlocal_ref, 1 - place_ref[0], scale, orbitals)


def second_kernel(
    place_ref, slab_ref, mate_ref, far_ref, proj_ref, own_msg, far_msg, beyond_msg, out_ref, *rest, orbitals, scale
):
    *chunk_refs, nonlocal_ref = rest
    coeff = atom_sums(own_msg[...], far_msg[...], beyond_msg[...])
    add_rest(out_ref, slab_ref, mate_ref, far_ref, proj_ref, coeff, nonlocal_ref, place_ref[0], scale, orbitals)
    share = ROWS // len(chunk_refs)
    for m, chunk_ref in enumerate(chunk_refs):
        at = (place_ref[1] ^ m) * share
        for i in range(share):
            chunk_ref[i] = row_of(out_ref, at + i, orbitals)


def gram_kernel(place_ref, *refs, orbitals, width, scale):
    *block_refs, out_ref, head_ref, tail_ref, gram_ref = refs
    for m, block_ref in enumerate(block_refs):
        at = pl.ds(pl.multiple_of((place_ref[1] ^ m) * orbitals, orbitals), orbitals)
        for i in range(block_ref.shape[0]):
            head, tail = two_parts(block_ref[i])
            head_ref[at, i * NX : (i + 1) * NX] = head
            tail_ref[at, i * NX : (i + 1) * NX] = tail
    head = head_ref[...]
    cross = dot_nt(tail_ref[...], head)
    gram_ref[...] = (dot_nt(head, head) + cross + cross.T) * scale
    n = gram_ref.shape[0]
    groups = len(block_refs)
    parts = [gram_ref[pl.ds(t, n // width, stride=width), :] for t in range(width)]
    lane = lanes(parts[0].shape)
    for q in range(groups):
        row = parts[0] if q == 0 else pltpu.roll(parts[0], n - orbitals * q, 1)
        for t in range(1, width):
            by = (orbitals * (t - q)) % n
            row = jnp.where(lane < orbitals * t, row, pltpu.roll(parts[t], by, 1) if by else parts[t])
        out_ref[pl.ds(q, n // width, stride=groups), :] = row


def params(mib):
    return pltpu.CompilerParams(vmem_limit_bytes=mib * 2**20)


def on_device(psi_in, v_local, proj_index, proj_value, kb_energy):
    orbitals = psi_in.shape[0]
    slabs = lax.axis_size("grid")
    groups = lax.axis_size("orb")
    mates = [(i, i ^ 1) for i in range(slabs)]
    fars = [(i, (i + 1 if i % 2 else i - 1) % slabs) for i in range(slabs)]
    n = orbitals * groups
    width = n // slabs

    def swap(x, pairs):
        return lax.ppermute(x, "grid", pairs)

    place = jnp.stack([lax.axis_index("grid") % 2, lax.axis_index("orb")]).astype(jnp.int32)
    field_shape = jax.ShapeDtypeStruct((orbitals * ROWS, NX), F32)
    message_shape = jax.ShapeDtypeStruct((orbitals, NX), F32)
    psi = psi_in.reshape(orbitals * ROWS, NX)
    v = v_local.reshape(ROWS, NX)
    kb = kb_energy.reshape(1, OWNED)
    kb = jnp.pad(kb, ((0, 0), (KAM, 0))) + jnp.zeros((1, KAM + OWNED), F32)
    kb = jnp.pad(jnp.concatenate([kb, kb[:, 2 * OWNED :]], axis=1), ((0, 0), (0, NX - 6 * OWNED)))

    def kernel(body, name, outs, scratch, mib, *operands, scalars=True, left=(), flops=10**9, **statics):
        return pl.pallas_call(
            functools.partial(body, **statics),
            out_shape=outs,
            in_specs=[SMEM] * scalars + [ANY if i in left else VMEM for i in range(len(operands))],
            out_specs=jax.tree.map(lambda _: VMEM, outs),
            scratch_shapes=scratch,
            compiler_params=params(mib),
            cost_estimate=pl.CostEstimate(flops=flops, bytes_accessed=10**7, transcendentals=0),
            name=name,
        )(*([place] * scalars), *operands)

    field_scratch = pltpu.VMEM((orbitals * ROWS, NX), F32)
    proj_shape = jax.ShapeDtypeStruct((ROWS, 3 * KAM, NX), BF16)
    proj_scratch = [pltpu.VMEM((2, ROWS * OWNED, SLOTS * PTS), BF16)]

    def slab(field, potential, scale, back, *start):
        scratch = [pltpu.VMEM((ROWS, NX), F32), field_scratch]
        return kernel(
            slab_kernel, "slab", field_shape, scratch, 8, field, potential, *start,
            scalars=False, orbitals=orbitals, scale=scale, back=back,
        )

    first_scale, scale = SIGMA / HALF_WIDTH, 2.0 * SIGMA_TWO / HALF_WIDTH
    far = swap(psi, fars)
    mate = swap(psi, mates)
    proj, own, to_mate = kernel(
        projector_kernel, "projectors", (proj_shape, message_shape, message_shape), proj_scratch, 16,
        proj_index, proj_value, kb, psi, orbitals=orbitals,
    )
    own = own + swap(to_mate, mates)
    values = proj_value.reshape(3 * OWNED, PTS)
    indices = proj_index.astype(F32).reshape(3 * SLOTS, PTS)
    value_at = orbitals + ROWS
    index_at = value_at + 3 * OWNED
    message = jnp.concatenate([own, v, values, indices], axis=0)
    from_far = swap(message, fars)
    message, field = lax.optimization_barrier((message, psi))
    local = slab(field, v, first_scale, None)
    local, mate = lax.optimization_barrier((local, mate))
    far_mate = swap(mate, fars)
    from_far, local = lax.optimization_barrier((from_far, local))
    from_beyond = swap(from_far, mates)
    first, own, to_mate, sums, far = kernel(
        first_kernel, "first", (field_shape, message_shape, message_shape, message_shape, field_shape),
        [field_scratch, pltpu.SemaphoreType.DMA(())], 16,
        local, mate, far, proj, message[:orbitals], from_far, from_beyond, kb,
        left=(2,), orbitals=orbitals, scale=first_scale,
    )
    first_mate = swap(first, mates)
    own = own + swap(to_mate, mates)
    far_again = swap(own, fars)
    own, from_far, far, first = lax.optimization_barrier((own, from_far, far, first))
    far_proj = kernel(
        far_projector_kernel, "far_projectors", proj_shape, proj_scratch, 16, from_far,
        index_at=index_at, value_at=value_at,
    )
    far_local = slab(far, from_far[orbitals:value_at], first_scale, None)
    local = slab(first, v, scale, -SIGMA * SIGMA_TWO, psi)
    far_again, far_proj, far_local, local = lax.optimization_barrier((far_again, far_proj, far_local, local))
    beyond_again = swap(far_again, mates)
    first_far = kernel(
        far_first_kernel, "far_first", field_shape, [field_scratch], 16,
        far_local, far_mate, psi, far_proj, sums, far_again, flops=20 * 10**8,
        orbitals=orbitals, scale=first_scale,
    )
    chunk = jax.ShapeDtypeStruct((ROWS // groups, orbitals, NX), F32)
    filtered, *blocks = kernel(
        second_kernel, "second", (field_shape,) + (chunk,) * groups, [field_scratch], 16,
        local, first_mate, first_far, proj, own, far_again, beyond_again, orbitals=orbitals, scale=scale,
    )
    for m in reversed(range(1, groups)):
        blocks[m] = lax.ppermute(blocks[m], "orb", [(i, i ^ m) for i in range(groups)])
    tiles = pl.pallas_call(
        functools.partial(gram_kernel, orbitals=orbitals, width=width, scale=1.0 / (slabs * ROWS * NX)),
        out_shape=jax.ShapeDtypeStruct((slabs * groups, n), F32),
        in_specs=[SMEM] + [VMEM] * groups,
        out_specs=VMEM,
        scratch_shapes=[pltpu.VMEM((n, ROWS // groups * NX), BF16)] * 2 + [pltpu.VMEM((n, n), F32)],
        compiler_params=params(8),
        cost_estimate=pl.CostEstimate(flops=10**8, bytes_accessed=10**6, transcendentals=0),
        name="gram",
    )(place, *blocks)
    tiles = lax.all_to_all(tiles, ("grid", "orb"), 0, 0, tiled=True)
    gram = jnp.sum(tiles, axis=0)[: width * orbitals].reshape(width, orbitals).T
    return filtered.reshape(psi_in.shape), gram


def solution(mesh):
    placed = (
        P("orb", "grid", None, None),
        P("grid", None, None),
        P("grid", None, None),
        P("grid", None, None, None),
        P("grid", None),
    )
    return jax.shard_map(
        on_device,
        mesh=mesh,
        in_specs=placed,
        out_specs=(P("orb", "grid", None, None), P("orb", "grid")),
        check_vma=False,
    )
```

```python
import functools

import jax
import jax.numpy as jnp
from jax import lax
from jax.experimental import pallas as pl
from jax.experimental.pallas import tpu as pltpu
from jax.sharding import PartitionSpec as P

LAP_COEF = (
    -5369.0 / 1800.0,
    12.0 / 7.0,
    -15.0 / 56.0,
    10.0 / 189.0,
    -1.0 / 112.0,
    2.0 / 1925.0,
    -1.0 / 16632.0,
)
HALF_WIDTH = 6.0
CENTRE = 8.0
SIGMA = HALF_WIDTH / (-3.0 - CENTRE)
SIGMA_TWO = 1.0 / (2.0 / SIGMA - SIGMA)

NX = 128
NY = 8
PLANES = 6
ROWS = PLANES * NY
SLOTS = 4
PROJ = 4
OWNED = SLOTS * PROJ
KAM = 3 * OWNED
PTS = 128

F32 = jnp.float32
BF16 = jnp.bfloat16
VMEM = pl.BlockSpec(memory_space=pltpu.VMEM)
SMEM = pl.BlockSpec(memory_space=pltpu.SMEM)
ANY = pl.BlockSpec(memory_space=pl.ANY)


def two_parts(x):
    head = x.astype(BF16)
    return head, (x - head.astype(F32)).astype(BF16)


def dot_nt(lhs, rhs):
    return lax.dot_general(lhs, rhs, (((1,), (1,)), ((), ())), preferred_element_type=F32)


def dot_nn(lhs, rhs):
    return lax.dot_general(lhs, rhs, (((1,), (0,)), ((), ())), preferred_element_type=F32)


def row_of(field_ref, row, orbitals):
    return field_ref[pl.ds(row, orbitals, stride=ROWS), :]


def lanes(shape):
    return lax.broadcasted_iota(jnp.int32, shape, 1)


def project(field_ref, proj_ref, orbitals):
    def step(pair, acc):
        row = 2 * pair
        points = jnp.concatenate([row_of(field_ref, row + i, orbitals) for i in (0, 1)], axis=1)
        head, tail = two_parts(points)
        lhs = jnp.concatenate([head, tail], axis=0)
        rhs = jnp.concatenate([proj_ref[row + i, :NX, :] for i in (0, 1)], axis=1)
        return acc + dot_nt(lhs, rhs)

    acc = lax.fori_loop(0, ROWS // 2, step, jnp.zeros((2 * orbitals, NX), F32), unroll=24)
    acc = acc[:orbitals] + acc[orbitals:]
    return jnp.where(lanes(acc.shape) < KAM, acc + pltpu.roll(acc, NX - KAM, 1), 0.0)


def put_messages(part, kb_ref, own_ref, mate_ref):
    lane = lanes(part.shape)
    kb = jnp.broadcast_to(kb_ref[...], part.shape)
    own_ref[...] = jnp.where(lane < KAM, part, jnp.where(lane < KAM + OWNED, kb, 0.0))
    mate = jnp.where(lane < 4 * OWNED, pltpu.roll(part, 3 * OWNED, 1), kb)
    mate = jnp.where(lane < 2 * OWNED, pltpu.roll(part, OWNED, 1), mate)
    mate = jnp.where(lane < 5 * OWNED, jnp.where(lane < 4 * OWNED, mate, pltpu.roll(part, 3 * OWNED, 1)), kb)
    sent = ((lane >= OWNED) & (lane < 2 * OWNED)) | ((lane >= 4 * OWNED) & (lane < 6 * OWNED))
    mate_ref[...] = jnp.where(sent, mate, 0.0)


def fill_projectors(even, index_of, value_of, proj_ref, lhs_ref):
    slot = lax.broadcasted_iota(jnp.int32, (OWNED, PTS), 0) // PROJ
    lane_no = lax.broadcasted_iota(jnp.int32, (NX, PTS), 0)
    row_no = lax.broadcasted_iota(jnp.int32, (ROWS, OWNED, PTS), 0)
    for frame in range(3):
        piece = frame + even * (2 - 2 * frame)
        index = index_of(piece)
        value = value_of(piece)
        parts = [p.astype(F32) for p in two_parts(value)]
        hits = []
        for a in range(SLOTS):
            mine = index[a : a + 1, :]
            row = jnp.where(slot == a, jnp.broadcast_to(mine >> 7, (OWNED, PTS)), -1)
            here = row_no == row[None]
            for i, part in enumerate(parts):
                chosen = jnp.where(here, part[None], 0.0)
                lhs_ref[i, :, a * PTS : (a + 1) * PTS] = chosen.reshape(ROWS * OWNED, PTS).astype(BF16)
            hits.append(jnp.where(lane_no == jnp.broadcast_to(mine & (NX - 1), (NX, PTS)), 1.0, 0.0).astype(BF16))
        rhs = jnp.concatenate(hits, axis=1)
        dense = dot_nt(lhs_ref[0], rhs) + dot_nt(lhs_ref[1], rhs)
        head, tail = two_parts(dense.reshape(ROWS, OWNED, NX))
        at = frame * OWNED
        proj_ref[:, at : at + OWNED, :] = head
        proj_ref[:, KAM + at : KAM + at + OWNED, :] = tail
        proj_ref[:, 2 * KAM + at : 2 * KAM + at + OWNED, :] = head


def projector_kernel(place_ref, index_ref, value_ref, kb_ref, psi_ref, proj_ref, own_ref, mate_ref, lhs_ref, *, orbitals):
    def value_of(piece):
        return jnp.concatenate([value_ref[piece, a] for a in range(SLOTS)], axis=0)

    fill_projectors(1 - place_ref[0], lambda piece: index_ref[piece], value_of, proj_ref, lhs_ref)
    put_messages(project(psi_ref, proj_ref, orbitals), kb_ref, own_ref, mate_ref)


def far_projector_kernel(place_ref, message_ref, proj_ref, lhs_ref, *, index_at, value_at):
    def index_of(piece):
        return message_ref[pl.ds(index_at + piece * SLOTS, SLOTS), :].astype(jnp.int32)

    def value_of(piece):
        return message_ref[pl.ds(pl.multiple_of(value_at + piece * OWNED, 8), OWNED), :]

    fill_projectors(place_ref[0], index_of, value_of, proj_ref, lhs_ref)


def weights(scale):
    return [-0.5 * scale * x for x in LAP_COEF]


def places(odd):
    return [NY * ((PLANES - 1 - j) + odd * (2 * j - PLANES + 1)) for j in range(PLANES)]


def banded(size, period, c):
    i, j = (lax.broadcasted_iota(jnp.int32, (size, size), d) for d in (0, 1))
    ahead = (j - i) & (period - 1)
    matrix = jnp.zeros((size, size), F32)
    for k in range(1, 7):
        for by in (k, -k):
            matrix = matrix + jnp.where(ahead == by % period, c[k], 0.0)
    return two_parts(jnp.where(i // period == j // period, matrix, 0.0))


def slab_kernel(field_ref, v_ref, *rest, orbitals, scale, back):
    start_ref = rest[0] if back is not None else None
    out_ref, v_scr, planar_ref = rest[-3:]
    v_scr[...] = (v_ref[...] - (CENTRE + 1.5 * LAP_COEF[0])) * scale
    c = weights(scale)
    head, tail = banded(NX, NX, c)
    along_x = jnp.concatenate(
        [jnp.concatenate([head, tail], axis=1), jnp.concatenate([head, jnp.zeros_like(tail)], axis=1)], axis=0
    )
    head, tail = banded(NX, NY, c)
    along_y = jnp.concatenate([head, head, tail], axis=1)

    def block(i, carry):
        at = pl.ds(pl.multiple_of(i * NX, NX), NX)
        head, tail = two_parts(field_ref[at, :])
        both = dot_nn(jnp.concatenate([head, tail], axis=1), along_x)
        across = dot_nn(along_y, jnp.concatenate([head, tail, head], axis=0))
        planar_ref[at, :] = both[:, :NX] + both[:, NX:] + across
        return carry

    lax.fori_loop(0, orbitals * ROWS // NX, block, 0, unroll=12)

    def orbital(o, carry):
        base = o * ROWS
        spots = [pl.ds(pl.multiple_of(base + NY * j, NY), NY) for j in range(PLANES)]
        cells = [field_ref[s, :] for s in spots]
        for j in range(PLANES):
            total = planar_ref[spots[j], :] + cells[j] * v_scr[NY * j : NY * j + NY, :]
            if back is not None:
                total = total + back * start_ref[spots[j], :]
            for k in range(1, PLANES):
                others = [cells[i] for i in (j - k, j + k) if 0 <= i < PLANES]
                if others:
                    total = total + c[k] * sum(others[1:], others[0])
            out_ref[spots[j], :] = total
        return carry

    lax.fori_loop(0, orbitals, orbital, 0, unroll=8)


def shift(x, by):
    return pltpu.roll(x, NX - by, 1)


def atom_sums(own, far, beyond):
    lane = lanes(own.shape)
    first, second = lane < OWNED, lane < 2 * OWNED
    sums = own + jnp.where(
        first,
        shift(own, 4 * OWNED) + shift(beyond, 2 * OWNED),
        jnp.where(second, shift(far, OWNED), pltpu.roll(far, OWNED, 1)),
    )
    energy = jnp.where(
        first, shift(own, 5 * OWNED), jnp.where(second, shift(own, 2 * OWNED), shift(far, OWNED))
    )
    return jnp.where(lane < KAM, sums * energy, 0.0)


def add_rest(
    out_ref, slab_ref, mate_ref, far_ref, proj_ref, coeff, nonlocal_ref, odd, scale, orbitals, until_here=None
):
    head, tail = two_parts((coeff * scale)[:, :KAM])
    lhs = jnp.concatenate([head, head, tail], axis=1)

    def spread(pair, carry):
        row = 2 * pair
        rhs = jnp.concatenate([proj_ref[row + i] for i in (0, 1)], axis=1)
        both = dot_nn(lhs, rhs)
        for i in (0, 1):
            nonlocal_ref[pl.ds(row + i, orbitals, stride=ROWS), :] = both[:, i * NX : (i + 1) * NX]
        return carry

    lax.fori_loop(0, ROWS // 2, spread, 0, unroll=24)
    if until_here is not None:
        until_here()
    c = weights(scale)
    place = places(odd)

    def orbital(o, carry):
        base = o * ROWS
        spots = [pl.ds(pl.multiple_of(base + p, NY), NY) for p in place]
        mate = [mate_ref[s, :] for s in spots]
        beyond = [far_ref[s, :] for s in spots]
        for j in range(PLANES):
            total = slab_ref[spots[j], :] + nonlocal_ref[spots[j], :]
            for k in range(1, 7):
                terms = []
                if j - k < 0:
                    terms.append(mate[PLANES + j - k])
                if j + k >= PLANES:
                    terms.append(beyond[j + k - PLANES])
                if terms:
                    total = total + c[k] * sum(terms[1:], terms[0])
            out_ref[spots[j], :] = total
        return carry

    lax.fori_loop(0, orbitals, orbital, 0, unroll=8)


def first_kernel(
    place_ref, slab_ref, mate_ref, far_arrived, proj_ref, own_msg, far_msg, beyond_msg, kb_ref,
    out_ref, own_out, mate_out, sums_ref, far_ref, nonlocal_ref, arrival, *, orbitals, scale,
):
    fetch = pltpu.make_async_copy(far_arrived, far_ref, arrival)
    fetch.start()
    sums = atom_sums(own_msg[...], far_msg[:orbitals, :], beyond_msg[:orbitals, :])
    sums_ref[...] = sums
    add_rest(
        out_ref, slab_ref, mate_ref, far_ref, proj_ref, sums, nonlocal_ref, place_ref[0], scale, orbitals, fetch.wait
    )
    put_messages(project(out_ref, proj_ref, orbitals), kb_ref, own_out, mate_out)
    lane = lanes(sums.shape)
    own_out[...] = jnp.where(lane < 6 * OWNED, own_out[...], jnp.where(lane < 7 * OWNED, pltpu.roll(sums, 6 * OWNED, 1), 0.0))


def far_first_kernel(
    place_ref, slab_ref, mate_ref, psi_ref, proj_ref, sums_ref, far_msg, out_ref, nonlocal_ref, *, orbitals, scale
):
    sums, far = sums_ref[...], far_msg[...]
    lane = lanes(sums.shape)
    far_sums = jnp.where(
        lane < OWNED, shift(far, 6 * OWNED), jnp.where(lane < 2 * OWNED, shift(sums, OWNED), pltpu.roll(sums, OWNED, 1))
    )
    add_rest(out_ref, slab_ref, mate_ref, psi_ref, proj_ref, far_sums, nonlocal_ref, 1 - place_ref[0], scale, orbitals)


def second_kernel(
    place_ref, slab_ref, mate_ref, far_ref, proj_ref, own_msg, far_msg, beyond_msg, out_ref, *rest, orbitals, scale
):
    *chunk_refs, nonlocal_ref = rest
    coeff = atom_sums(own_msg[...], far_msg[...], beyond_msg[...])
    add_rest(out_ref, slab_ref, mate_ref, far_ref, proj_ref, coeff, nonlocal_ref, place_ref[0], scale, orbitals)
    share = ROWS // len(chunk_refs)
    for m, chunk_ref in enumerate(chunk_refs):
        at = (place_ref[1] ^ m) * share
        for i in range(share):
            chunk_ref[i] = row_of(out_ref, at + i, orbitals)


def gram_kernel(place_ref, *refs, orbitals, width, scale):
    *block_refs, out_ref, head_ref, tail_ref, gram_ref = refs
    for m, block_ref in enumerate(block_refs):
        at = pl.ds(pl.multiple_of((place_ref[1] ^ m) * orbitals, orbitals), orbitals)
        for i in range(block_ref.shape[0]):
            head, tail = two_parts(block_ref[i])
            head_ref[at, i * NX : (i + 1) * NX] = head
            tail_ref[at, i * NX : (i + 1) * NX] = tail
    head = head_ref[...]
    cross = dot_nt(tail_ref[...], head)
    gram_ref[...] = (dot_nt(head, head) + cross + cross.T) * scale
    n = gram_ref.shape[0]
    groups = len(block_refs)
    parts = [gram_ref[pl.ds(t, n // width, stride=width), :] for t in range(width)]
    lane = lanes(parts[0].shape)
    for q in range(groups):
        row = parts[0] if q == 0 else pltpu.roll(parts[0], n - orbitals * q, 1)
        for t in range(1, width):
            by = (orbitals * (t - q)) % n
            row = jnp.where(lane < orbitals * t, row, pltpu.roll(parts[t], by, 1) if by else parts[t])
        out_ref[pl.ds(q, n // width, stride=groups), :] = row


def params(mib):
    return pltpu.CompilerParams(vmem_limit_bytes=mib * 2**20)


def on_device(psi_in, v_local, proj_index, proj_value, kb_energy):
    orbitals = psi_in.shape[0]
    slabs = lax.axis_size("grid")
    groups = lax.axis_size("orb")
    mates = [(i, i ^ 1) for i in range(slabs)]
    fars = [(i, (i + 1 if i % 2 else i - 1) % slabs) for i in range(slabs)]
    n = orbitals * groups
    width = n // slabs

    def swap(x, pairs):
        return lax.ppermute(x, "grid", pairs)

    place = jnp.stack([lax.axis_index("grid") % 2, lax.axis_index("orb")]).astype(jnp.int32)
    field_shape = jax.ShapeDtypeStruct((orbitals * ROWS, NX), F32)
    message_shape = jax.ShapeDtypeStruct((orbitals, NX), F32)
    psi = psi_in.reshape(orbitals * ROWS, NX)
    v = v_local.reshape(ROWS, NX)
    kb = kb_energy.reshape(1, OWNED)
    kb = jnp.pad(kb, ((0, 0), (KAM, 0))) + jnp.zeros((1, KAM + OWNED), F32)
    kb = jnp.pad(jnp.concatenate([kb, kb[:, 2 * OWNED :]], axis=1), ((0, 0), (0, NX - 6 * OWNED)))

    def kernel(body, name, outs, scratch, mib, *operands, scalars=True, left=(), flops=10**9, **statics):
        return pl.pallas_call(
            functools.partial(body, **statics),
            out_shape=outs,
            in_specs=[SMEM] * scalars + [ANY if i in left else VMEM for i in range(len(operands))],
            out_specs=jax.tree.map(lambda _: VMEM, outs),
            scratch_shapes=scratch,
            compiler_params=params(mib),
            cost_estimate=pl.CostEstimate(flops=flops, bytes_accessed=10**7, transcendentals=0),
            name=name,
        )(*([place] * scalars), *operands)

    field_scratch = pltpu.VMEM((orbitals * ROWS, NX), F32)
    proj_shape = jax.ShapeDtypeStruct((ROWS, 3 * KAM, NX), BF16)
    proj_scratch = [pltpu.VMEM((2, ROWS * OWNED, SLOTS * PTS), BF16)]

    def slab(field, potential, scale, back, *start):
        scratch = [pltpu.VMEM((ROWS, NX), F32), field_scratch]
        return kernel(
            slab_kernel, "slab", field_shape, scratch, 8, field, potential, *start,
            scalars=False, orbitals=orbitals, scale=scale, back=back,
        )

    first_scale, scale = SIGMA / HALF_WIDTH, 2.0 * SIGMA_TWO / HALF_WIDTH
    far = swap(psi, fars)
    mate = swap(psi, mates)
    proj, own, to_mate = kernel(
        projector_kernel, "projectors", (proj_shape, message_shape, message_shape), proj_scratch, 16,
        proj_index, proj_value, kb, psi, orbitals=orbitals,
    )
    own = own + swap(to_mate, mates)
    values = proj_value.reshape(3 * OWNED, PTS)
    indices = proj_index.astype(F32).reshape(3 * SLOTS, PTS)
    value_at = orbitals + ROWS
    index_at = value_at + 3 * OWNED
    message = jnp.concatenate([own, v, values, indices], axis=0)
    from_far = swap(message, fars)
    message, field = lax.optimization_barrier((message, psi))
    local = slab(field, v, first_scale, None)
    local, mate = lax.optimization_barrier((local, mate))
    far_mate = swap(mate, fars)
    from_far, local = lax.optimization_barrier((from_far, local))
    from_beyond = swap(from_far, mates)
    first, own, to_mate, sums, far = kernel(
        first_kernel, "first", (field_shape, message_shape, message_shape, message_shape, field_shape),
        [field_scratch, pltpu.SemaphoreType.DMA(())], 16,
        local, mate, far, proj, message[:orbitals], from_far, from_beyond, kb,
        left=(2,), orbitals=orbitals, scale=first_scale,
    )
    first_mate = swap(first, mates)
    own = own + swap(to_mate, mates)
    far_again = swap(own, fars)
    own, from_far, far, first = lax.optimization_barrier((own, from_far, far, first))
    far_proj = kernel(
        far_projector_kernel, "far_projectors", proj_shape, proj_scratch, 16, from_far,
        index_at=index_at, value_at=value_at,
    )
    far_local = slab(far, from_far[orbitals:value_at], first_scale, None)
    local = slab(first, v, scale, -SIGMA * SIGMA_TWO, psi)
    far_again, far_proj, far_local, local = lax.optimization_barrier((far_again, far_proj, far_local, local))
    beyond_again = swap(far_again, mates)
    first_far = kernel(
        far_first_kernel, "far_first", field_shape, [field_scratch], 16,
        far_local, far_mate, psi, far_proj, sums, far_again, flops=20 * 10**8,
        orbitals=orbitals, scale=first_scale,
    )
    chunk = jax.ShapeDtypeStruct((ROWS // groups, orbitals, NX), F32)
    filtered, *blocks = kernel(
        second_kernel, "second", (field_shape,) + (chunk,) * groups, [field_scratch], 16,
        local, first_mate, first_far, proj, own, far_again, beyond_again, orbitals=orbitals, scale=scale,
    )
    for m in reversed(range(1, groups)):
        blocks[m] = lax.ppermute(blocks[m], "orb", [(i, i ^ m) for i in range(groups)])
    tiles = pl.pallas_call(
        functools.partial(gram_kernel, orbitals=orbitals, width=width, scale=1.0 / (slabs * ROWS * NX)),
        out_shape=jax.ShapeDtypeStruct((slabs * groups, n), F32),
        in_specs=[SMEM] + [VMEM] * groups,
        out_specs=VMEM,
        scratch_shapes=[pltpu.VMEM((n, ROWS // groups * NX), BF16)] * 2 + [pltpu.VMEM((n, n), F32)],
        compiler_params=params(8),
        cost_estimate=pl.CostEstimate(flops=10**8, bytes_accessed=10**6, transcendentals=0),
        name="gram",
    )(place, *blocks)
    tiles = lax.all_to_all(tiles, ("grid", "orb"), 0, 0, tiled=True)
    gram = jnp.sum(tiles, axis=0)[: width * orbitals].reshape(width, orbitals).T
    return filtered.reshape(psi_in.shape), gram


def solution(mesh):
    placed = (
        P("orb", "grid", None, None),
        P("grid", None, None),
        P("grid", None, None),
        P("grid", None, None, None),
        P("grid", None),
    )
    return jax.shard_map(
        on_device,
        mesh=mesh,
        in_specs=placed,
        out_specs=(P("orb", "grid", None, None), P("orb", "grid")),
        check_vma=False,
    )
```
